32 devices in a mesh: ctx: 4 (over y, x), tp: 8 (over z, core).
Axes of the slice: x: 2, y: 2, z: 4, core: 2. Of those that a mesh axis runs over, the one named last changes fastest.
Arguments:
- grad_out: bfloat16 [512, 5120], P('ctx', 'tp'), may hold values from -6 to 6
- w_out: bfloat16 [1024, 5120], P('tp'), may hold values from -0.078125 to 0.078125
- query_proj: bfloat16 [512, 1024], P('ctx', 'tp'), may hold values from -6 to 6
- key_proj: bfloat16 [512, 1024], P('ctx', 'tp'), may hold values from -6 to 6
- value_proj: bfloat16 [512, 1024], P('ctx', 'tp'), may hold values from -6 to 6
- w_query: bfloat16 [5120, 1024], P(None, 'tp'), may hold values from -0.25 to 0.25
- w_key: bfloat16 [5120, 1024], P(None, 'tp'), may hold values from -0.1875 to 0.1875
- w_value: bfloat16 [5120, 1024], P(None, 'tp'), may hold values from -0.1875 to 0.1875
- tile_keys: int32 [4, 3], replicated, may hold values from 0 to 3, as said below
Outputs:
- input_grad: float32 [5120, 512], P('tp', 'ctx')
The draws below stay inside these ranges and needn't reach their ends.
Inputs may be any that keep to these rules, and one draw needn't show every extreme that they name: `tile_keys`: each row lists 3 distinct key tiles, among them the query tile itself; every listed tile u has |u - t| <= 2 for its query tile t.
All inputs are finite; a program needn't handle non-finite values.
Results may differ from the reference program's by a relative error of at most 0.0078.
Values may be sent and summed in bfloat16 or wider, within the bound.
No kernel may reach another device: no remote copies, remote signals or barrier semaphores. Data moves between devices by JAX's collectives and lax.ppermute only.
A program may use at most 64 MiB of HBM per device.

```python
import jax
import jax.numpy as jnp
from jax import lax

D = 5120
HD = 128
TILE = 128
TILES_DEV = 1
HEADS = 8
TILES = 4
TOKENS = 512
REACH = 2
KEEP = 3


def drawn_pair(key):
    base = jax.random.fold_in(key, 11)
    key_query, key_keys = jax.random.split(base, 2)
    shape = (TOKENS, HEADS * HD)
    queries = jnp.clip(jax.random.normal(key_query, shape, jnp.float32), -6.0, 6.0)
    keys_out = jnp.clip(jax.random.normal(key_keys, shape, jnp.float32), -6.0, 6.0)
    return (queries, keys_out)


def draw_query_proj(key, part):
    return drawn_pair(key)[0].astype(jnp.bfloat16)


def draw_key_proj(key, part):
    return drawn_pair(key)[1].astype(jnp.bfloat16)


def draw_tile_keys(key, part):
    tile_ids = jnp.arange(TILES, dtype=jnp.int32)
    time_rows = tile_ids // TILES_DEV
    inside = jnp.abs(time_rows[:, None] - time_rows[None, :]) <= REACH
    noise = jax.random.randint(jax.random.fold_in(key, 23), (TILES, TILES), 0, 2 ** 20)
    ranking = noise * TILES + tile_ids[None, :]
    ranking = jnp.where(inside, ranking, -1 - tile_ids[None, :])
    ranking = jnp.where(tile_ids[:, None] == tile_ids[None, :], 2 ** 30 + tile_ids[None, :], ranking)
    _, picked = lax.top_k(ranking, KEEP)
    return picked.astype(jnp.int32)


def spiked(values, stream_key, source, target, parts, factor):
    owner, partner = [(jnp.arange(values.shape[position]) // (values.shape[position] // parts)).reshape([-1 if axis == position else 1 for axis in range(values.ndim)]) for position in (source, target)]
    chosen = jax.random.permutation(stream_key, parts)[partner]
    strong = (owner == chosen) | (owner == (partner + parts // 2) % parts)
    return jnp.where(strong, factor * values, values)


def steps_of(stream_key, extent, cuts, low, largest):
    def one(axis_at, blocks):
        draws = jax.random.uniform(jax.random.fold_in(jax.random.fold_in(stream_key, 6), axis_at), (blocks,), jnp.float32, low / len(cuts), largest / len(cuts))
        return jnp.repeat(jnp.exp(draws), extent[axis_at] // blocks).reshape((-1,) + (1,) * (len(extent) - axis_at - 1))

    gain = one(*cuts[0])
    for cut in cuts[1:]:
        gain = gain * one(*cut)
    return gain


def gaussian(stream_key, shape, width, bound, cuts=(), held_as=jnp.bfloat16):
    loudness = steps_of(stream_key, shape, cuts, -0.22, 0.18) if cuts else 1.0
    drawn = jax.random.normal(stream_key, shape, jnp.float32) * width * loudness
    return jnp.minimum(jnp.maximum(drawn, -bound), bound).astype(held_as)


def heavy_noise(own_key, dims, width, most, cuts, heavy, kind=jnp.bfloat16):
    drawn = width * jax.random.normal(own_key, dims, jnp.float32)
    if cuts:
        drawn = drawn * steps_of(own_key, dims, cuts, -0.22, 0.18)
    return jnp.clip(spiked(drawn, jax.random.fold_in(own_key, 3), *heavy), -most, most).astype(kind)


def setup_inputs(seed: int = 0) -> dict:
    keys = jax.random.split(jax.random.key(seed), 10)
    return {
        "grad_out": gaussian(keys[0], (TOKENS, D), 1.0, 6.0, ((0, 4), (1, 8))),
        "w_out": gaussian(keys[1], (HEADS * HD, D), D ** -0.5, 0.078125, ((0, 8),)),
        "query_proj": draw_query_proj(jax.random.fold_in(keys[9], 71), 0),
        "key_proj": draw_key_proj(jax.random.fold_in(keys[9], 71), 0),
        "value_proj": gaussian(keys[4], (TOKENS, HEADS * HD), 1.0, 6.0, ((0, 4), (1, 8))),
        "w_query": heavy_noise(keys[5], (D, HEADS * HD), (HEADS * HD) ** -0.5, 0.25, ((1, 8),), (1, 0, 8, 2.0)),
        "w_key": gaussian(keys[6], (D, HEADS * HD), (HEADS * HD) ** -0.5, 0.1875, ((1, 8),)),
        "w_value": gaussian(keys[7], (D, HEADS * HD), (HEADS * HD) ** -0.5, 0.1875, ((1, 8),)),
        "tile_keys": draw_tile_keys(jax.random.fold_in(keys[9], 71), 0),
    }


def head_gradient(head_index, grad_out, w_out, query_proj, key_proj, value_proj, w_query, w_key, w_value, token_mask):
    score_scale = HD ** -0.5
    head_start = head_index * HD
    out_rows = lax.dynamic_slice_in_dim(w_out, head_start, HD, 0)
    d_attn = lax.dot_general(grad_out, out_rows, (((1,), (1,)), ((), ())), preferred_element_type=jnp.float32).astype(jnp.bfloat16)
    queries = lax.dynamic_slice_in_dim(query_proj, head_start, HD, 1)
    keys_head = lax.dynamic_slice_in_dim(key_proj, head_start, HD, 1)
    values_head = lax.dynamic_slice_in_dim(value_proj, head_start, HD, 1)
    scores = lax.dot_general(queries, keys_head, (((1,), (1,)), ((), ())), preferred_element_type=jnp.float32) * score_scale
    scores = jnp.where(token_mask, scores, -jnp.inf)
    row_max = jnp.max(scores, axis=1, keepdims=True)
    exponent = jnp.exp(scores - row_max)
    row_total = jnp.sum(exponent, axis=1, keepdims=True)
    prob_exact = exponent / row_total
    prob_half = prob_exact.astype(jnp.bfloat16)
    attn_out = jnp.dot(prob_half, values_head, preferred_element_type=jnp.float32)
    row_delta = jnp.sum(d_attn.astype(jnp.float32) * attn_out, axis=1, keepdims=True)
    d_prob = lax.dot_general(d_attn, values_head, (((1,), (1,)), ((), ())), preferred_element_type=jnp.float32)
    d_score = (prob_exact * (d_prob - row_delta) * score_scale).astype(jnp.bfloat16)
    d_query = jnp.dot(d_score, keys_head, preferred_element_type=jnp.float32).astype(jnp.bfloat16)
    d_key = lax.dot_general(d_score, queries, (((0,), (0,)), ((), ())), preferred_element_type=jnp.float32).astype(jnp.bfloat16)
    d_value = lax.dot_general(prob_half, d_attn, (((0,), (0,)), ((), ())), preferred_element_type=jnp.float32).astype(jnp.bfloat16)
    query_cols = lax.dynamic_slice_in_dim(w_query, head_start, HD, 1)
    key_cols = lax.dynamic_slice_in_dim(w_key, head_start, HD, 1)
    value_cols = lax.dynamic_slice_in_dim(w_value, head_start, HD, 1)
    contract = (((1,), (1,)), ((), ()))
    head_term = lax.dot_general(query_cols, d_query, contract, preferred_element_type=jnp.float32)
    head_term = head_term + lax.dot_general(key_cols, d_key, contract, preferred_element_type=jnp.float32)
    head_term = head_term + lax.dot_general(value_cols, d_value, contract, preferred_element_type=jnp.float32)
    return head_term


def reference(grad_out, w_out, query_proj, key_proj, value_proj, w_query, w_key, w_value, tile_keys):
    tile_ids = jnp.arange(TILES, dtype=jnp.int32)
    tile_ok = jnp.any(tile_keys[:, :, None] == tile_ids[None, None, :], axis=1)
    token_mask = jnp.repeat(jnp.repeat(tile_ok, TILE, axis=0), TILE, axis=1)

    def scan_step(running, head_index):
        head_term = head_gradient(head_index, grad_out, w_out, query_proj, key_proj, value_proj, w_query, w_key, w_value, token_mask)
        return running + head_term, None

    running, _ = lax.scan(scan_step, jnp.zeros((D, TOKENS), jnp.float32), jnp.arange(HEADS, dtype=jnp.int32))
    return running
```

```python
import functools

import jax
import jax.numpy as jnp
from jax import lax
from jax.experimental import pallas as pl
from jax.experimental.pallas import tpu as pltpu
from jax.sharding import PartitionSpec as P

TILE = 128
CONTRACT_LAST = (((1,), (1,)), ((), ()))
CONTRACT_FIRST = (((0,), (0,)), ((), ()))
VMEM = pl.BlockSpec(memory_space=pltpu.VMEM)
SMEM = pl.BlockSpec(memory_space=pltpu.SMEM)


def dot_f32(a, b, dims):
    return lax.dot_general(a, b, dims, preferred_element_type=jnp.float32)


def many_slabs(
    grad_out, w_out, query_proj, key_proj, value_proj, w_query, w_key, w_value, tile_keys
):
    row_count = query_proj.shape[0]
    head_size = query_proj.shape[1]
    score_scale = head_size ** (-0.5)
    tiles_here = row_count // TILE
    slab_index = lax.axis_index("ctx")
    d_attn = dot_f32(
        lax.all_gather(grad_out, "tp", axis=1, tiled=True), w_out, CONTRACT_LAST
    ).astype(jnp.bfloat16)
    keys_all, values_all = (
        lax.all_gather(key_proj, "ctx", axis=0, tiled=True),
        lax.all_gather(value_proj, "ctx", axis=0, tiled=True),
    )
    total_tiles = keys_all.shape[0] // TILE
    own_lists = lax.dynamic_slice_in_dim(tile_keys, slab_index * tiles_here, tiles_here, 0)
    all_tiles = jnp.arange(total_tiles, dtype=jnp.int32)
    tile_ok = jnp.any(own_lists[:, :, None] == all_tiles[None, None, :], axis=1)
    token_mask = jnp.repeat(jnp.repeat(tile_ok, TILE, axis=0), TILE, axis=1)
    scores = dot_f32(query_proj, keys_all, CONTRACT_LAST) * score_scale
    scores = jnp.where(token_mask, scores, -jnp.inf)
    row_max = jnp.max(scores, axis=1, keepdims=True)
    exponent = jnp.exp(scores - row_max)
    row_total = jnp.sum(exponent, axis=1, keepdims=True)
    prob_exact = exponent / row_total
    prob_half = prob_exact.astype(jnp.bfloat16)
    attn_out = jnp.dot(prob_half, values_all, preferred_element_type=jnp.float32)
    row_delta = jnp.sum(d_attn.astype(jnp.float32) * attn_out, axis=1, keepdims=True)
    d_prob = dot_f32(d_attn, values_all, CONTRACT_LAST)
    d_score = (prob_exact * (d_prob - row_delta) * score_scale).astype(jnp.bfloat16)
    d_query = jnp.dot(d_score, keys_all, preferred_element_type=jnp.float32).astype(jnp.bfloat16)
    key_part = dot_f32(d_score, query_proj, CONTRACT_FIRST)
    value_part = dot_f32(prob_half, d_attn, CONTRACT_FIRST)
    key_sums = lax.psum_scatter(
        jnp.concatenate([key_part, value_part], axis=1), "ctx", scatter_dimension=0, tiled=True
    )
    d_key = key_sums[:, :head_size].astype(jnp.bfloat16)
    d_value = key_sums[:, head_size:].astype(jnp.bfloat16)
    feature_sum = dot_f32(w_query, d_query, CONTRACT_LAST)
    feature_sum = feature_sum + dot_f32(w_key, d_key, CONTRACT_LAST)
    feature_sum = feature_sum + dot_f32(w_value, d_value, CONTRACT_LAST)
    return lax.psum_scatter(feature_sum, "tp", scatter_dimension=0, tiled=True)


def attn_grad_kernel(chips, cols, pos_ref, *refs):
    blocks = refs[:chips]
    own_w, mate_w, own_ref, mate_ref = refs[chips:]
    chip, core = pos_ref[0], pos_ref[1]
    own = jnp.zeros(own_ref.shape, jnp.float32)
    mate = jnp.zeros(own_ref.shape, jnp.float32)
    for step in range(chips):
        start = pl.multiple_of(((chip ^ step) * 2 + core) * cols, 128)
        block = blocks[step][...]
        own = own + dot_f32(block, own_w[:, pl.ds(start, cols)], CONTRACT_LAST)
        mate = mate + dot_f32(block, mate_w[:, pl.ds(start, cols)], CONTRACT_LAST)
    own_ref[...] = own
    mate_ref[...] = mate


def softmax_kernel(slabs, keep, pos_ref, lists_ref, *refs):
    packs = refs[:slabs]
    row_ref, col_ref, attn_ref = refs[slabs:]
    rows = packs[0].shape[0]
    size = packs[0].shape[1] // 3
    tiles = rows // TILE
    slab = pos_ref[2]
    scale = size ** (-0.5)
    keys = jnp.concatenate([pack[:, size : 2 * size] for pack in packs], axis=0)
    values = jnp.concatenate([pack[:, 2 * size :] for pack in packs], axis=0)
    for turn in range(slabs):
        for tile in range(tiles):
            query_tile = (slab ^ turn) * tiles + tile
            span = pl.ds(turn * rows + tile * TILE, TILE)
            scores = dot_f32(packs[turn][pl.ds(tile * TILE, TILE), :size], keys, CONTRACT_LAST)
            scores = scores * scale
            parts = []
            for other in range(slabs * tiles):
                key_tile = (slab ^ (other // tiles)) * tiles + other % tiles
                listed = lists_ref[query_tile, 0] == key_tile
                for place in range(1, keep):
                    listed = listed | (lists_ref[query_tile, place] == key_tile)
                part = scores[:, other * TILE : (other + 1) * TILE]
                parts.append(jnp.where(listed, part, -jnp.inf))
            scores = jnp.concatenate(parts, axis=1)
            exponent = jnp.exp(scores - jnp.max(scores, axis=1, keepdims=True))
            prob = exponent / jnp.sum(exponent, axis=1, keepdims=True)
            attn_ref[span, :] = jnp.dot(
                prob.astype(jnp.bfloat16), values, preferred_element_type=jnp.float32
            )
            col_ref[span, :] = prob[:, :rows]
            if turn == 0:
                row_ref[pl.ds(tile * TILE, TILE), :] = prob


def query_grad_kernel(slabs, grad_ref, *refs):
    packs = refs[:slabs]
    row_ref, attn_ref, out_ref = refs[slabs:]
    rows = packs[0].shape[0]
    size = packs[0].shape[1] // 3
    scale = size ** (-0.5)
    grad = grad_ref[...]
    keys = jnp.concatenate([pack[:, size : 2 * size] for pack in packs], axis=0)
    values = jnp.concatenate([pack[:, 2 * size :] for pack in packs], axis=0)
    delta = jnp.sum(grad.astype(jnp.float32) * attn_ref[:rows, :], axis=1, keepdims=True)
    d_prob = dot_f32(grad, values, CONTRACT_LAST)
    d_score = (row_ref[...] * (d_prob - delta) * scale).astype(jnp.bfloat16)
    out_ref[...] = jnp.dot(d_score, keys, preferred_element_type=jnp.float32).astype(jnp.bfloat16)


def key_grad_kernel(slabs, *refs):
    grads = refs[:slabs]
    packs = refs[slabs : 2 * slabs]
    query_ref, col_ref, attn_ref, out_ref = refs[2 * slabs :]
    size = packs[0].shape[1] // 3
    scale = size ** (-0.5)
    queries = jnp.concatenate([pack[:, :size] for pack in packs], axis=0)
    grad = jnp.concatenate([part[...] for part in grads], axis=0)
    prob = col_ref[...]
    delta = jnp.sum(grad.astype(jnp.float32) * attn_ref[...], axis=1, keepdims=True)
    d_prob = dot_f32(grad, packs[0][:, 2 * size :], CONTRACT_LAST)
    d_score = (prob * (d_prob - delta) * scale).astype(jnp.bfloat16)
    out_ref[:, :size] = query_ref[...]
    out_ref[:, size : 2 * size] = dot_f32(d_score, queries, CONTRACT_FIRST).astype(jnp.bfloat16)
    out_ref[:, 2 * size :] = dot_f32(prob.astype(jnp.bfloat16), grad, CONTRACT_FIRST).astype(
        jnp.bfloat16
    )


def project_kernel(rows, step, pos_ref, own_ref, mate_ref, *refs):
    weights, out_ref = refs[:6], refs[6]
    start = pl.multiple_of(((pos_ref[0] ^ step) * 2 + pos_ref[1]) * rows, 16)
    size = own_ref.shape[1] // 3
    total = None
    for place, weight in enumerate(weights):
        grads = own_ref if place < 3 else mate_ref
        part = grads[:, (place % 3) * size : (place % 3 + 1) * size]
        term = dot_f32(weight[pl.ds(start, rows), :], part, CONTRACT_LAST)
        total = term if total is None else total + term
    out_ref[...] = total.astype(out_ref.dtype)


def sum_kernel(own_ref, *refs):
    total = own_ref[...]
    for part in refs[:-1]:
        total = total + part[...].astype(jnp.float32)
    refs[-1][...] = total


def call(kernel, ins, outs):
    return pl.pallas_call(
        kernel,
        in_specs=ins,
        out_specs=[VMEM] * len(outs),
        out_shape=[jax.ShapeDtypeStruct(shape, kind) for shape, kind in outs],
    )


def few_slabs(
    slabs,
    chips,
    grad_out,
    w_out,
    query_proj,
    key_proj,
    value_proj,
    w_query,
    w_key,
    w_value,
    tile_keys,
):
    rows, cols = grad_out.shape
    size = query_proj.shape[1]
    half, full = jnp.bfloat16, jnp.float32
    tp_index = lax.axis_index("tp")
    pos = jnp.stack([tp_index // 2, tp_index % 2, lax.axis_index("ctx")]).astype(jnp.int32)

    def to_chip(x, step):
        return lax.ppermute(x, "tp", [(t, t ^ (2 * step)) for t in range(2 * chips)])

    def to_mate(x):
        return lax.ppermute(x, "tp", [(t, t ^ 1) for t in range(2 * chips)])

    def to_slab(x, turn):
        return lax.ppermute(x, "ctx", [(c, c ^ turn) for c in range(slabs)])

    blocks = [grad_out] + [to_chip(grad_out, step) for step in range(1, chips)]
    mate_out = to_mate(w_out)
    pack = jnp.concatenate([query_proj, key_proj, value_proj], axis=1)
    packs = [pack] + [to_slab(pack, turn) for turn in range(1, slabs)]
    own_w = [w_query, w_key, w_value]
    mate_w = [to_mate(w) for w in own_w]

    prob_row, prob_col, attn_out = call(
        functools.partial(softmax_kernel, slabs, tile_keys.shape[1]),
        [SMEM, SMEM] + [VMEM] * slabs,
        [((rows, slabs * rows), full), ((slabs * rows, rows), full), ((slabs * rows, size), full)],
    )(pos, tile_keys, *packs)

    own_part, mate_part = call(
        functools.partial(attn_grad_kernel, chips, cols),
        [SMEM] + [VMEM] * (chips + 2),
        [((rows, size), full), ((rows, size), full)],
    )(pos, *blocks, w_out, mate_out)
    grad = (own_part + to_mate(mate_part)).astype(half)
    grads = [grad] + [to_slab(grad, turn) for turn in range(1, slabs)]

    (d_query,) = call(
        functools.partial(query_grad_kernel, slabs),
        [VMEM] * (slabs + 3),
        [((rows, size), half)],
    )(grad, *packs, prob_row, attn_out)
    (own_grads,) = call(
        functools.partial(key_grad_kernel, slabs),
        [VMEM] * (2 * slabs + 3),
        [((rows, 3 * size), half)],
    )(*grads, *packs, d_query, prob_col, attn_out)
    mate_grads = to_mate(own_grads)

    arrived = []
    order = sorted(range(1, chips), reverse=True)
    for step in order + [0]:
        (part,) = call(
            functools.partial(project_kernel, cols, step),
            [SMEM] + [VMEM] * 8,
            [((cols, rows), half if step else full)],
        )(pos, own_grads, mate_grads, *own_w, *mate_w)
        if step:
            arrived.append(to_chip(part, step))
    (out,) = call(sum_kernel, [VMEM] * chips, [((cols, rows), full)])(part, *arrived)
    return out


def solution(mesh):
    slabs, shards = mesh.shape["ctx"], mesh.shape["tp"]
    chips = shards // 2
    few = slabs <= 8 and slabs & (slabs - 1) == 0
    few = few and shards == 2 * chips and chips <= 8 and chips & (chips - 1) == 0
    return jax.shard_map(
        functools.partial(few_slabs, slabs, chips) if few else many_slabs,
        mesh=mesh,
        in_specs=(
            P("ctx", "tp"),
            P("tp", None),
            P("ctx", "tp"),
            P("ctx", "tp"),
            P("ctx", "tp"),
            P(None, "tp"),
            P(None, "tp"),
            P(None, "tp"),
            P(),
        ),
        out_specs=P("tp", "ctx"),
        check_vma=False,
    )
```

```python
import functools

import jax
import jax.numpy as jnp
from jax import lax
from jax.experimental import pallas as pl
from jax.experimental.pallas import tpu as pltpu
from jax.sharding import PartitionSpec as P


TILE = 128
CONTRACT_LAST = (((1,), (1,)), ((), ()))
CONTRACT_FIRST = (((0,), (0,)), ((), ()))
VMEM = pl.BlockSpec(memory_space=pltpu.VMEM)
SMEM = pl.BlockSpec(memory_space=pltpu.SMEM)


def dot_f32(a, b, dims):
    return lax.dot_general(a, b, dims, preferred_element_type=jnp.float32)


def many_slabs(
    grad_out, w_out, query_proj, key_proj, value_proj, w_query, w_key, w_value, tile_keys
):
    row_count = query_proj.shape[0]
    head_size = query_proj.shape[1]
    score_scale = head_size ** (-0.5)
    tiles_here = row_count // TILE
    slab_index = lax.axis_index("ctx")
    d_attn = dot_f32(
        lax.all_gather(grad_out, "tp", axis=1, tiled=True), w_out, CONTRACT_LAST
    ).astype(jnp.bfloat16)
    keys_all, values_all = (
        lax.all_gather(key_proj, "ctx", axis=0, tiled=True),
        lax.all_gather(value_proj, "ctx", axis=0, tiled=True),
    )
    total_tiles = keys_all.shape[0] // TILE
    own_lists = lax.dynamic_slice_in_dim(tile_keys, slab_index * tiles_here, tiles_here, 0)
    all_tiles = jnp.arange(total_tiles, dtype=jnp.int32)
    tile_ok = jnp.any(own_lists[:, :, None] == all_tiles[None, None, :], axis=1)
    token_mask = jnp.repeat(jnp.repeat(tile_ok, TILE, axis=0), TILE, axis=1)
    scores = dot_f32(query_proj, keys_all, CONTRACT_LAST) * score_scale
    scores = jnp.where(token_mask, scores, -jnp.inf)
    row_max = jnp.max(scores, axis=1, keepdims=True)
    exponent = jnp.exp(scores - row_max)
    row_total = jnp.sum(exponent, axis=1, keepdims=True)
    prob_exact = exponent / row_total
    prob_half = prob_exact.astype(jnp.bfloat16)
    attn_out = jnp.dot(prob_half, values_all, preferred_element_type=jnp.float32)
    row_delta = jnp.sum(d_attn.astype(jnp.float32) * attn_out, axis=1, keepdims=True)
    d_prob = dot_f32(d_attn, values_all, CONTRACT_LAST)
    d_score = (prob_exact * (d_prob - row_delta) * score_scale).astype(jnp.bfloat16)
    d_query = jnp.dot(d_score, keys_all, preferred_element_type=jnp.float32).astype(jnp.bfloat16)
    key_part = dot_f32(d_score, query_proj, CONTRACT_FIRST)
    value_part = dot_f32(prob_half, d_attn, CONTRACT_FIRST)
    key_sums = lax.psum_scatter(
        jnp.concatenate([key_part, value_part], axis=1), "ctx", scatter_dimension=0, tiled=True
    )
    d_key = key_sums[:, :head_size].astype(jnp.bfloat16)
    d_value = key_sums[:, head_size:].astype(jnp.bfloat16)
    feature_sum = dot_f32(w_query, d_query, CONTRACT_LAST)
    feature_sum = feature_sum + dot_f32(w_key, d_key, CONTRACT_LAST)
    feature_sum = feature_sum + dot_f32(w_value, d_value, CONTRACT_LAST)
    return lax.psum_scatter(feature_sum, "tp", scatter_dimension=0, tiled=True)


def pack_kernel(query_ref, key_ref, value_ref, out_ref):
    size = query_ref.shape[1]
    out_ref[:, :size] = query_ref[...]
    out_ref[:, size : 2 * size] = key_ref[...]
    out_ref[:, 2 * size :] = value_ref[...]


def attn_grad_kernel(chips, cols, *refs):
    blocks = refs[:chips]
    own_w, mate_w, own_ref, mate_ref = refs[chips:]
    index = lax.axis_index("tp")
    own = jnp.zeros(own_ref.shape, jnp.float32)
    mate = jnp.zeros(own_ref.shape, jnp.float32)
    for step in range(chips):
        start = pl.multiple_of((index ^ (2 * step)) * cols, 128)
        block = blocks[step][...]
        own = own + dot_f32(block, own_w[:, pl.ds(start, cols)], CONTRACT_LAST)
        mate = mate + dot_f32(block, mate_w[:, pl.ds(start, cols)], CONTRACT_LAST)
    own_ref[...] = own
    mate_ref[...] = mate


def softmax_kernel(slabs, keep, lists_ref, *refs):
    packs = refs[:slabs]
    row_ref, col_ref, attn_ref = refs[slabs:]
    rows = packs[0].shape[0]
    size = packs[0].shape[1] // 3
    tiles = rows // TILE
    slab = lax.axis_index("ctx")
    scale = size ** (-0.5)
    keys = jnp.concatenate([pack[:, size : 2 * size] for pack in packs], axis=0)
    values = jnp.concatenate([pack[:, 2 * size :] for pack in packs], axis=0)
    for turn in range(slabs):
        for tile in range(tiles):
            query_tile = (slab ^ turn) * tiles + tile
            span = pl.ds(turn * rows + tile * TILE, TILE)
            scores = dot_f32(packs[turn][pl.ds(tile * TILE, TILE), :size], keys, CONTRACT_LAST)
            scores = scores * scale
            parts = []
            for other in range(slabs * tiles):
                key_tile = (slab ^ (other // tiles)) * tiles + other % tiles
                listed = lists_ref[query_tile, 0] == key_tile
                for place in range(1, keep):
                    listed = listed | (lists_ref[query_tile, place] == key_tile)
                part = scores[:, other * TILE : (other + 1) * TILE]
                parts.append(jnp.where(listed, part, -jnp.inf))
            scores = jnp.concatenate(parts, axis=1)
            exponent = jnp.exp(scores - jnp.max(scores, axis=1, keepdims=True))
            prob = exponent / jnp.sum(exponent, axis=1, keepdims=True)
            attn_ref[span, :] = jnp.dot(
                prob.astype(jnp.bfloat16), values, preferred_element_type=jnp.float32
            )
            col_ref[span, :] = prob[:, :rows]
            if turn == 0:
                row_ref[pl.ds(tile * TILE, TILE), :] = prob


def query_grad_kernel(slabs, grad_ref, *refs):
    packs = refs[:slabs]
    row_ref, attn_ref, out_ref = refs[slabs:]
    rows = packs[0].shape[0]
    size = packs[0].shape[1] // 3
    scale = size ** (-0.5)
    grad = grad_ref[...]
    keys = jnp.concatenate([pack[:, size : 2 * size] for pack in packs], axis=0)
    values = jnp.concatenate([pack[:, 2 * size :] for pack in packs], axis=0)
    delta = jnp.sum(grad.astype(jnp.float32) * attn_ref[:rows, :], axis=1, keepdims=True)
    d_prob = dot_f32(grad, values, CONTRACT_LAST)
    d_score = (row_ref[...] * (d_prob - delta) * scale).astype(jnp.bfloat16)
    out_ref[...] = jnp.dot(d_score, keys, preferred_element_type=jnp.float32).astype(jnp.bfloat16)


def key_grad_kernel(slabs, *refs):
    grads = refs[:slabs]
    packs = refs[slabs : 2 * slabs]
    query_ref, col_ref, attn_ref, out_ref = refs[2 * slabs :]
    size = packs[0].shape[1] // 3
    scale = size ** (-0.5)
    queries = jnp.concatenate([pack[:, :size] for pack in packs], axis=0)
    grad = jnp.concatenate([part[...] for part in grads], axis=0)
    prob = col_ref[...]
    delta = jnp.sum(grad.astype(jnp.float32) * attn_ref[...], axis=1, keepdims=True)
    d_prob = dot_f32(grad, packs[0][:, 2 * size :], CONTRACT_LAST)
    d_score = (prob * (d_prob - delta) * scale).astype(jnp.bfloat16)
    out_ref[:, :size] = query_ref[...]
    out_ref[:, size : 2 * size] = dot_f32(d_score, queries, CONTRACT_FIRST).astype(jnp.bfloat16)
    out_ref[:, 2 * size :] = dot_f32(prob.astype(jnp.bfloat16), grad, CONTRACT_FIRST).astype(
        jnp.bfloat16
    )


def project_kernel(rows, step, own_ref, mate_ref, *refs):
    weights, out_ref = refs[:6], refs[6]
    start = pl.multiple_of((lax.axis_index("tp") ^ (2 * step)) * rows, 16)
    size = own_ref.shape[1] // 3
    total = None
    for place, weight in enumerate(weights):
        grads = own_ref if place < 3 else mate_ref
        part = grads[:, (place % 3) * size : (place % 3 + 1) * size]
        term = dot_f32(weight[pl.ds(start, rows), :], part, CONTRACT_LAST)
        total = term if total is None else total + term
    out_ref[...] = total.astype(out_ref.dtype)


def sum_kernel(own_ref, *refs):
    total = own_ref[...]
    for part in refs[:-1]:
        total = total + part[...].astype(jnp.float32)
    refs[-1][...] = total


def call(kernel, args, outs, fast_out=True):
    ints = [x.dtype == jnp.int32 for x in args]
    args = [
        x if flag else pltpu.with_memory_space_constraint(x, pltpu.VMEM)
        for x, flag in zip(args, ints)
    ]
    return pl.pallas_call(
        kernel,
        in_specs=[SMEM if flag else VMEM for flag in ints],
        out_specs=[VMEM] * len(outs),
        out_shape=[
            pltpu.VMEM(shape, kind) if fast_out else jax.ShapeDtypeStruct(shape, kind)
            for shape, kind in outs
        ],
        compiler_params=pltpu.CompilerParams(vmem_limit_bytes=16 << 20),
    )(*args)


def few_slabs(
    slabs,
    chips,
    grad_out,
    w_out,
    query_proj,
    key_proj,
    value_proj,
    w_query,
    w_key,
    w_value,
    tile_keys,
):
    rows, cols = grad_out.shape
    size = query_proj.shape[1]
    half, full = jnp.bfloat16, jnp.float32
    hops = sorted(range(1, chips), key=lambda step: (step & (step - 1) != 0, -step))

    def to_chip(x, step):
        return lax.ppermute(x, "tp", [(t, t ^ (2 * step)) for t in range(2 * chips)])

    def to_mate(x):
        return lax.ppermute(x, "tp", [(t, t ^ 1) for t in range(2 * chips)])

    def to_slab(x, turn):
        return lax.ppermute(x, "ctx", [(c, c ^ turn) for c in range(slabs)])

    blocks = [grad_out] + [to_chip(grad_out, step) for step in range(1, chips)]
    (pack,) = call(pack_kernel, [query_proj, key_proj, value_proj], [((rows, 3 * size), half)])
    packs = [pack] + [to_slab(pack, turn) for turn in range(1, slabs)]
    mate_out = to_mate(w_out)
    own_w = [w_query, w_key, w_value]
    mate_w = [to_mate(w) for w in own_w]

    prob_row, prob_col, attn_out = call(
        functools.partial(softmax_kernel, slabs, tile_keys.shape[1]),
        [tile_keys, *packs],
        [((rows, slabs * rows), full), ((slabs * rows, rows), full), ((slabs * rows, size), full)],
    )
    own_part, mate_part = call(
        functools.partial(attn_grad_kernel, chips, cols),
        [*blocks, w_out, mate_out],
        [((rows, size), full), ((rows, size), full)],
    )
    grad = (own_part + to_mate(mate_part)).astype(half)
    grads = [grad] + [to_slab(grad, turn) for turn in range(1, slabs)]
    (d_query,) = call(
        functools.partial(query_grad_kernel, slabs),
        [grad, *packs, prob_row, attn_out],
        [((rows, size), half)],
    )
    (own_grads,) = call(
        functools.partial(key_grad_kernel, slabs),
        [*grads, *packs, d_query, prob_col, attn_out],
        [((rows, 3 * size), half)],
    )
    mate_grads = to_mate(own_grads)
    arrived = []
    for step in hops + [0]:
        (part,) = call(
            functools.partial(project_kernel, cols, step),
            [own_grads, mate_grads, *own_w, *mate_w],
            [((cols, rows), half if step else full)],
        )
        if step:
            arrived.append(to_chip(part, step))
    (out,) = call(sum_kernel, [part, *arrived], [((cols, rows), full)], fast_out=False)
    return out


def solution(mesh):
    slabs, shards = mesh.shape["ctx"], mesh.shape["tp"]
    chips = shards // 2
    few = 1 < slabs <= 8 and slabs & (slabs - 1) == 0
    few = few and shards == 2 * chips and 2 <= chips <= 8 and chips & (chips - 1) == 0
    return jax.shard_map(
        functools.partial(few_slabs, slabs, chips) if few else many_slabs,
        mesh=mesh,
        in_specs=(
            P("ctx", "tp"),
            P("tp", None),
            P("ctx", "tp"),
            P("ctx", "tp"),
            P("ctx", "tp"),
            P(None, "tp"),
            P(None, "tp"),
            P(None, "tp"),
            P(),
        ),
        out_specs=P("tp", "ctx"),
        check_vma=False,
    )
```

```python
import functools

import jax
import jax.numpy as jnp
from jax import lax
from jax.experimental import pallas as pl
from jax.experimental.pallas import tpu as pltpu
from jax.sharding import PartitionSpec as P


TILE = 128
CONTRACT_LAST = (((1,), (1,)), ((), ()))
CONTRACT_FIRST = (((0,), (0,)), ((), ()))
VMEM = pl.BlockSpec(memory_space=pltpu.VMEM)
SMEM = pl.BlockSpec(memory_space=pltpu.SMEM)


def dot_f32(a, b, dims):
    return lax.dot_general(a, b, dims, preferred_element_type=jnp.float32)


def many_slabs(
    grad_out, w_out, query_proj, key_proj, value_proj, w_query, w_key, w_value, tile_keys
):
    row_count = query_proj.shape[0]
    head_size = query_proj.shape[1]
    score_scale = head_size ** (-0.5)
    tiles_here = row_count // TILE
    slab_index = lax.axis_index("ctx")
    d_attn = dot_f32(
        lax.all_gather(grad_out, "tp", axis=1, tiled=True), w_out, CONTRACT_LAST
    ).astype(jnp.bfloat16)
    keys_all, values_all = (
        lax.all_gather(key_proj, "ctx", axis=0, tiled=True),
        lax.all_gather(value_proj, "ctx", axis=0, tiled=True),
    )
    total_tiles = keys_all.shape[0] // TILE
    own_lists = lax.dynamic_slice_in_dim(tile_keys, slab_index * tiles_here, tiles_here, 0)
    all_tiles = jnp.arange(total_tiles, dtype=jnp.int32)
    tile_ok = jnp.any(own_lists[:, :, None] == all_tiles[None, None, :], axis=1)
    token_mask = jnp.repeat(jnp.repeat(tile_ok, TILE, axis=0), TILE, axis=1)
    scores = dot_f32(query_proj, keys_all, CONTRACT_LAST) * score_scale
    scores = jnp.where(token_mask, scores, -jnp.inf)
    row_max = jnp.max(scores, axis=1, keepdims=True)
    exponent = jnp.exp(scores - row_max)
    row_total = jnp.sum(exponent, axis=1, keepdims=True)
    prob_exact = exponent / row_total
    prob_half = prob_exact.astype(jnp.bfloat16)
    attn_out = jnp.dot(prob_half, values_all, preferred_element_type=jnp.float32)
    row_delta = jnp.sum(d_attn.astype(jnp.float32) * attn_out, axis=1, keepdims=True)
    d_prob = dot_f32(d_attn, values_all, CONTRACT_LAST)
    d_score = (prob_exact * (d_prob - row_delta) * score_scale).astype(jnp.bfloat16)
    d_query = jnp.dot(d_score, keys_all, preferred_element_type=jnp.float32).astype(jnp.bfloat16)
    key_part = dot_f32(d_score, query_proj, CONTRACT_FIRST)
    value_part = dot_f32(prob_half, d_attn, CONTRACT_FIRST)
    key_sums = lax.psum_scatter(
        jnp.concatenate([key_part, value_part], axis=1), "ctx", scatter_dimension=0, tiled=True
    )
    d_key = key_sums[:, :head_size].astype(jnp.bfloat16)
    d_value = key_sums[:, head_size:].astype(jnp.bfloat16)
    feature_sum = dot_f32(w_query, d_query, CONTRACT_LAST)
    feature_sum = feature_sum + dot_f32(w_key, d_key, CONTRACT_LAST)
    feature_sum = feature_sum + dot_f32(w_value, d_value, CONTRACT_LAST)
    return lax.psum_scatter(feature_sum, "tp", scatter_dimension=0, tiled=True)


def pack_kernel(query_ref, key_ref, value_ref, out_ref, sems):
    size = query_ref.shape[1]
    copies = [
        pltpu.make_async_copy(
            part, out_ref.at[:, place * size : (place + 1) * size], sems.at[place]
        )
        for place, part in enumerate((query_ref, key_ref, value_ref))
    ]
    for copy in copies:
        copy.start()
    for copy in copies:
        copy.wait()


def fetch_kernel(count, *refs):
    sems = refs[2 * count]
    copies = [
        pltpu.make_async_copy(refs[place], refs[count + place], sems.at[place])
        for place in range(count)
    ]
    for copy in copies:
        copy.start()
    for copy in copies:
        copy.wait()


def is_inner():
    chip = lax.axis_index("tp") >> 1
    return (chip == 1) | (chip == 2)


def attn_grad_kernel(cols, own_block, near, cross_in, cross_out, mid, relay, own_w, mate_w, own_ref, mate_ref):
    index = lax.axis_index("tp")
    inner = is_inner()
    blocks = [
        own_block[...],
        near[...],
        jnp.where(inner, cross_in[...], cross_out[...]),
        jnp.where(inner, mid[...], relay[...]),
    ]
    own = jnp.zeros(own_ref.shape, jnp.float32)
    mate = jnp.zeros(own_ref.shape, jnp.float32)
    for step, block in enumerate(blocks):
        start = pl.multiple_of((index ^ (2 * step)) * cols, 128)
        own = own + dot_f32(block, own_w[:, pl.ds(start, cols)], CONTRACT_LAST)
        mate = mate + dot_f32(block, mate_w[:, pl.ds(start, cols)], CONTRACT_LAST)
    own_ref[...] = own
    mate_ref[...] = mate


def softmax_kernel(slabs, keep, lists_ref, *refs):
    packs = refs[:slabs]
    row_ref, col_ref, attn_ref = refs[slabs:]
    rows = packs[0].shape[0]
    size = packs[0].shape[1] // 3
    tiles = rows // TILE
    slab = lax.axis_index("ctx")
    scale = size ** (-0.5)
    keys = jnp.concatenate([pack[:, size : 2 * size] for pack in packs], axis=0)
    values = jnp.concatenate([pack[:, 2 * size :] for pack in packs], axis=0)
    for turn in range(slabs):
        for tile in range(tiles):
            query_tile = (slab ^ turn) * tiles + tile
            span = pl.ds(turn * rows + tile * TILE, TILE)
            scores = dot_f32(packs[turn][pl.ds(tile * TILE, TILE), :size], keys, CONTRACT_LAST)
            scores = scores * scale
            parts = []
            for other in range(slabs * tiles):
                key_tile = (slab ^ (other // tiles)) * tiles + other % tiles
                listed = lists_ref[query_tile, 0] == key_tile
                for place in range(1, keep):
                    listed = listed | (lists_ref[query_tile, place] == key_tile)
                part = scores[:, other * TILE : (other + 1) * TILE]
                parts.append(jnp.where(listed, part, -jnp.inf))
            scores = jnp.concatenate(parts, axis=1)
            exponent = jnp.exp(scores - jnp.max(scores, axis=1, keepdims=True))
            prob = exponent / jnp.sum(exponent, axis=1, keepdims=True)
            attn_ref[span, :] = jnp.dot(
                prob.astype(jnp.bfloat16), values, preferred_element_type=jnp.float32
            )
            col_ref[span, :] = prob[:, :rows]
            if turn == 0:
                row_ref[pl.ds(tile * TILE, TILE), :] = prob


def query_grad_kernel(slabs, grad_ref, *refs):
    packs = refs[:slabs]
    row_ref, attn_ref, out_ref = refs[slabs:]
    rows = packs[0].shape[0]
    size = packs[0].shape[1] // 3
    scale = size ** (-0.5)
    grad = grad_ref[...]
    keys = jnp.concatenate([pack[:, size : 2 * size] for pack in packs], axis=0)
    values = jnp.concatenate([pack[:, 2 * size :] for pack in packs], axis=0)
    delta = jnp.sum(grad.astype(jnp.float32) * attn_ref[:rows, :], axis=1, keepdims=True)
    d_prob = dot_f32(grad, values, CONTRACT_LAST)
    d_score = (row_ref[...] * (d_prob - delta) * scale).astype(jnp.bfloat16)
    out_ref[...] = jnp.dot(d_score, keys, preferred_element_type=jnp.float32).astype(jnp.bfloat16)


def key_grad_kernel(slabs, *refs):
    grads = refs[:slabs]
    packs = refs[slabs : 2 * slabs]
    query_ref, col_ref, attn_ref, out_ref = refs[2 * slabs :]
    size = packs[0].shape[1] // 3
    scale = size ** (-0.5)
    queries = jnp.concatenate([pack[:, :size] for pack in packs], axis=0)
    grad = jnp.concatenate([part[...] for part in grads], axis=0)
    prob = col_ref[...]
    delta = jnp.sum(grad.astype(jnp.float32) * attn_ref[...], axis=1, keepdims=True)
    d_prob = dot_f32(grad, packs[0][:, 2 * size :], CONTRACT_LAST)
    d_score = (prob * (d_prob - delta) * scale).astype(jnp.bfloat16)
    out_ref[:, :size] = query_ref[...]
    out_ref[:, size : 2 * size] = dot_f32(d_score, queries, CONTRACT_FIRST).astype(jnp.bfloat16)
    out_ref[:, 2 * size :] = dot_f32(prob.astype(jnp.bfloat16), grad, CONTRACT_FIRST).astype(
        jnp.bfloat16
    )


def project_kernel(rows, step, own_ref, mate_ref, *refs):
    weights, out_ref = refs[:6], refs[-1]
    start = pl.multiple_of((lax.axis_index("tp") ^ (2 * step)) * rows, 16)
    size = own_ref.shape[1] // 3
    total = None
    for place, weight in enumerate(weights):
        grads = own_ref if place < 3 else mate_ref
        part = grads[:, (place % 3) * size : (place % 3 + 1) * size]
        term = dot_f32(weight[pl.ds(start, rows), :], part, CONTRACT_LAST)
        total = term if total is None else total + term
    for fed in refs[6:-1]:
        total = total + fed[...].astype(jnp.float32)
    out_ref[...] = total.astype(out_ref.dtype)


def sum_kernel(own_ref, near, cross_in, cross_out, mid, out_ref):
    full = jnp.float32
    total = own_ref[...] + near[...].astype(full)
    through = cross_in[...].astype(full) + mid[...].astype(full)
    out_ref[...] = total + jnp.where(is_inner(), through, cross_out[...].astype(full))


def call(kernel, args, outs, fast_out=True, raw=False, sems=0):
    ints = [x.dtype == jnp.int32 for x in args]
    space = pltpu.HBM if raw else pltpu.VMEM
    args = [
        x if flag else pltpu.with_memory_space_constraint(x, space) for x, flag in zip(args, ints)
    ]
    there = pl.BlockSpec(memory_space=space)
    return pl.pallas_call(
        kernel,
        in_specs=[SMEM if flag else there for flag in ints],
        out_specs=[VMEM] * len(outs),
        out_shape=[
            pltpu.VMEM(shape, kind) if fast_out else jax.ShapeDtypeStruct(shape, kind)
            for shape, kind in outs
        ],
        scratch_shapes=[pltpu.SemaphoreType.DMA((sems,))] if sems else [],
        compiler_params=pltpu.CompilerParams(vmem_limit_bytes=16 << 20),
    )(*args)


FEED = ((0, 1), (3, 2))
RELAY = ((2, 3), (1, 0))
CROSS_IN = ((0, 2), (3, 1))
CROSS_OUT = ((2, 0), (1, 3))
MID = ((1, 2), (2, 1))
NEAR = ((0, 1), (1, 0), (2, 3), (3, 2))


def few_slabs(
    slabs,
    grad_out,
    w_out,
    query_proj,
    key_proj,
    value_proj,
    w_query,
    w_key,
    w_value,
    tile_keys,
):
    rows, cols = grad_out.shape
    size = query_proj.shape[1]
    half, full = jnp.bfloat16, jnp.float32

    def along(x, way):
        pairs = [(2 * a + core, 2 * b + core) for a, b in way for core in range(2)]
        return lax.ppermute(x, "tp", pairs)

    def to_mate(x):
        return lax.ppermute(x, "tp", [(t, t ^ 1) for t in range(8)])

    def to_slab(x, turn):
        return lax.ppermute(x, "ctx", [(c, c ^ turn) for c in range(slabs)])

    g_in = along(grad_out, CROSS_IN)
    g_near = along(grad_out, NEAR)
    g_out = along(grad_out, CROSS_OUT)
    g_mid = along(grad_out, MID)
    g_relay = along(g_in, RELAY)
    (pack,) = call(
        pack_kernel, [query_proj, key_proj, value_proj], [((rows, 3 * size), half)],
        raw=True, sems=3,
    )
    packs = [pack] + [to_slab(pack, turn) for turn in range(1, slabs)]
    mate_out = to_mate(w_out)
    own_w = [w_query, w_key, w_value]
    mate_w = [to_mate(w) for w in own_w]
    near_out, near_grad = call(
        functools.partial(fetch_kernel, 2), [w_out, grad_out],
        [(w_out.shape, half), (grad_out.shape, half)], raw=True, sems=2,
    )
    prob_row, prob_col, attn_out = call(
        functools.partial(softmax_kernel, slabs, tile_keys.shape[1]),
        [tile_keys, *packs],
        [((rows, slabs * rows), full), ((slabs * rows, rows), full), ((slabs * rows, size), full)],
    )
    own_part, mate_part = call(
        functools.partial(attn_grad_kernel, cols),
        [near_grad, g_near, g_in, g_out, g_mid, g_relay, near_out, mate_out],
        [((rows, size), full), ((rows, size), full)],
    )
    grad = (own_part + to_mate(mate_part)).astype(half)
    grads = [grad] + [to_slab(grad, turn) for turn in range(1, slabs)]
    (d_query,) = call(
        functools.partial(query_grad_kernel, slabs),
        [grad, *packs, prob_row, attn_out],
        [((rows, size), half)],
    )
    (own_grads,) = call(
        functools.partial(key_grad_kernel, slabs),
        [*grads, *packs, d_query, prob_col, attn_out],
        [((rows, 3 * size), half)],
    )
    mate_grads = to_mate(own_grads)

    def project(step, kind, *fed):
        (part,) = call(
            functools.partial(project_kernel, cols, step),
            [own_grads, mate_grads, *own_w, *mate_w, *fed],
            [((cols, rows), kind)],
        )
        return part

    third, second = project(3, half), project(2, half)
    fed = along(third, FEED)
    f_in = along(second, CROSS_IN)
    f_mid = along(third, MID)
    f_near = along(project(1, half), NEAR)
    f_out = along(project(2, half, fed), CROSS_OUT)
    (out,) = call(
        sum_kernel,
        [project(0, full), f_near, f_in, f_out, f_mid],
        [((cols, rows), full)],
        fast_out=False,
    )
    return out


def solution(mesh):
    slabs, shards = mesh.shape["ctx"], mesh.shape["tp"]
    few = slabs in (4, 8) and shards == 8
    return jax.shard_map(
        functools.partial(few_slabs, slabs) if few else many_slabs,
        mesh=mesh,
        in_specs=(
            P("ctx", "tp"),
            P("tp", None),
            P("ctx", "tp"),
            P("ctx", "tp"),
            P("ctx", "tp"),
            P(None, "tp"),
            P(None, "tp"),
            P(None, "tp"),
            P(),
        ),
        out_specs=P("tp", "ctx"),
        check_vma=False,
    )
```

```python
import functools

import jax
import jax.numpy as jnp
from jax import lax
from jax.experimental import pallas as pl
from jax.experimental.pallas import tpu as pltpu
from jax.sharding import PartitionSpec as P


TILE = 128
CONTRACT_LAST = (((1,), (1,)), ((), ()))
CONTRACT_FIRST = (((0,), (0,)), ((), ()))
VMEM = pl.BlockSpec(memory_space=pltpu.VMEM)
SMEM = pl.BlockSpec(memory_space=pltpu.SMEM)


def dot_f32(a, b, dims):
    return lax.dot_general(a, b, dims, preferred_element_type=jnp.float32)


def many_slabs(
    grad_out, w_out, query_proj, key_proj, value_proj, w_query, w_key, w_value, tile_keys
):
    row_count = query_proj.shape[0]
    head_size = query_proj.shape[1]
    score_scale = head_size ** (-0.5)
    tiles_here = row_count // TILE
    slab_index = lax.axis_index("ctx")
    d_attn = dot_f32(
        lax.all_gather(grad_out, "tp", axis=1, tiled=True), w_out, CONTRACT_LAST
    ).astype(jnp.bfloat16)
    keys_all, values_all = (
        lax.all_gather(key_proj, "ctx", axis=0, tiled=True),
        lax.all_gather(value_proj, "ctx", axis=0, tiled=True),
    )
    total_tiles = keys_all.shape[0] // TILE
    own_lists = lax.dynamic_slice_in_dim(tile_keys, slab_index * tiles_here, tiles_here, 0)
    all_tiles = jnp.arange(total_tiles, dtype=jnp.int32)
    tile_ok = jnp.any(own_lists[:, :, None] == all_tiles[None, None, :], axis=1)
    token_mask = jnp.repeat(jnp.repeat(tile_ok, TILE, axis=0), TILE, axis=1)
    scores = dot_f32(query_proj, keys_all, CONTRACT_LAST) * score_scale
    scores = jnp.where(token_mask, scores, -jnp.inf)
    row_max = jnp.max(scores, axis=1, keepdims=True)
    exponent = jnp.exp(scores - row_max)
    row_total = jnp.sum(exponent, axis=1, keepdims=True)
    prob_exact = exponent / row_total
    prob_half = prob_exact.astype(jnp.bfloat16)
    attn_out = jnp.dot(prob_half, values_all, preferred_element_type=jnp.float32)
    row_delta = jnp.sum(d_attn.astype(jnp.float32) * attn_out, axis=1, keepdims=True)
    d_prob = dot_f32(d_attn, values_all, CONTRACT_LAST)
    d_score = (prob_exact * (d_prob - row_delta) * score_scale).astype(jnp.bfloat16)
    d_query = jnp.dot(d_score, keys_all, preferred_element_type=jnp.float32).astype(jnp.bfloat16)
    key_part = dot_f32(d_score, query_proj, CONTRACT_FIRST)
    value_part = dot_f32(prob_half, d_attn, CONTRACT_FIRST)
    key_sums = lax.psum_scatter(
        jnp.concatenate([key_part, value_part], axis=1), "ctx", scatter_dimension=0, tiled=True
    )
    d_key = key_sums[:, :head_size].astype(jnp.bfloat16)
    d_value = key_sums[:, head_size:].astype(jnp.bfloat16)
    feature_sum = dot_f32(w_query, d_query, CONTRACT_LAST)
    feature_sum = feature_sum + dot_f32(w_key, d_key, CONTRACT_LAST)
    feature_sum = feature_sum + dot_f32(w_value, d_value, CONTRACT_LAST)
    return lax.psum_scatter(feature_sum, "tp", scatter_dimension=0, tiled=True)


def pack_kernel(query_ref, key_ref, value_ref, out_ref, sems):
    size = query_ref.shape[1]
    copies = [
        pltpu.make_async_copy(
            part, out_ref.at[:, place * size : (place + 1) * size], sems.at[place]
        )
        for place, part in enumerate((query_ref, key_ref, value_ref))
    ]
    for copy in copies:
        copy.start()
    for copy in copies:
        copy.wait()


def fetch_kernel(count, *refs):
    sems = refs[2 * count]
    copies = [
        pltpu.make_async_copy(refs[place], refs[count + place], sems.at[place])
        for place in range(count)
    ]
    for copy in copies:
        copy.start()
    for copy in copies:
        copy.wait()


def attn_grad_kernel(chips, cols, *refs):
    blocks = refs[:chips]
    own_w, mate_w, own_ref, mate_ref = refs[chips:]
    index = lax.axis_index("tp")
    own = jnp.zeros(own_ref.shape, jnp.float32)
    mate = jnp.zeros(own_ref.shape, jnp.float32)
    for step in range(chips):
        start = pl.multiple_of((index ^ (2 * step)) * cols, 128)
        block = blocks[step][...]
        own = own + dot_f32(block, own_w[:, pl.ds(start, cols)], CONTRACT_LAST)
        mate = mate + dot_f32(block, mate_w[:, pl.ds(start, cols)], CONTRACT_LAST)
    own_ref[...] = own
    mate_ref[...] = mate


def softmax_kernel(slabs, keep, lists_ref, *refs):
    packs = refs[:slabs]
    row_ref, col_ref, attn_ref = refs[slabs:]
    rows = packs[0].shape[0]
    size = packs[0].shape[1] // 3
    tiles = rows // TILE
    slab = lax.axis_index("ctx")
    scale = size ** (-0.5)
    keys = jnp.concatenate([pack[:, size : 2 * size] for pack in packs], axis=0)
    values = jnp.concatenate([pack[:, 2 * size :] for pack in packs], axis=0)
    for turn in range(slabs):
        for tile in range(tiles):
            query_tile = (slab ^ turn) * tiles + tile
            span = pl.ds(turn * rows + tile * TILE, TILE)
            scores = dot_f32(packs[turn][pl.ds(tile * TILE, TILE), :size], keys, CONTRACT_LAST)
            scores = scores * scale
            parts = []
            for other in range(slabs * tiles):
                key_tile = (slab ^ (other // tiles)) * tiles + other % tiles
                listed = lists_ref[query_tile, 0] == key_tile
                for place in range(1, keep):
                    listed = listed | (lists_ref[query_tile, place] == key_tile)
                part = scores[:, other * TILE : (other + 1) * TILE]
                parts.append(jnp.where(listed, part, -jnp.inf))
            scores = jnp.concatenate(parts, axis=1)
            exponent = jnp.exp(scores - jnp.max(scores, axis=1, keepdims=True))
            prob = exponent / jnp.sum(exponent, axis=1, keepdims=True)
            attn_ref[span, :] = jnp.dot(
                prob.astype(jnp.bfloat16), values, preferred_element_type=jnp.float32
            )
            col_ref[span, :] = prob[:, :rows]
            if turn == 0:
                row_ref[pl.ds(tile * TILE, TILE), :] = prob


def query_grad_kernel(slabs, grad_ref, *refs):
    packs = refs[:slabs]
    row_ref, attn_ref, out_ref = refs[slabs:]
    rows = packs[0].shape[0]
    size = packs[0].shape[1] // 3
    scale = size ** (-0.5)
    grad = grad_ref[...]
    keys = jnp.concatenate([pack[:, size : 2 * size] for pack in packs], axis=0)
    values = jnp.concatenate([pack[:, 2 * size :] for pack in packs], axis=0)
    delta = jnp.sum(grad.astype(jnp.float32) * attn_ref[:rows, :], axis=1, keepdims=True)
    d_prob = dot_f32(grad, values, CONTRACT_LAST)
    d_score = (row_ref[...] * (d_prob - delta) * scale).astype(jnp.bfloat16)
    out_ref[...] = jnp.dot(d_score, keys, preferred_element_type=jnp.float32).astype(jnp.bfloat16)


def key_grad_kernel(slabs, *refs):
    grads = refs[:slabs]
    packs = refs[slabs : 2 * slabs]
    query_ref, col_ref, attn_ref, out_ref = refs[2 * slabs :]
    size = packs[0].shape[1] // 3
    scale = size ** (-0.5)
    queries = jnp.concatenate([pack[:, :size] for pack in packs], axis=0)
    grad = jnp.concatenate([part[...] for part in grads], axis=0)
    prob = col_ref[...]
    delta = jnp.sum(grad.astype(jnp.float32) * attn_ref[...], axis=1, keepdims=True)
    d_prob = dot_f32(grad, packs[0][:, 2 * size :], CONTRACT_LAST)
    d_score = (prob * (d_prob - delta) * scale).astype(jnp.bfloat16)
    out_ref[:, :size] = query_ref[...]
    out_ref[:, size : 2 * size] = dot_f32(d_score, queries, CONTRACT_FIRST).astype(jnp.bfloat16)
    out_ref[:, 2 * size :] = dot_f32(prob.astype(jnp.bfloat16), grad, CONTRACT_FIRST).astype(
        jnp.bfloat16
    )


def project_kernel(rows, step, own_ref, mate_ref, *refs):
    weights, out_ref = refs[:6], refs[-1]
    start = pl.multiple_of((lax.axis_index("tp") ^ (2 * step)) * rows, 16)
    size = own_ref.shape[1] // 3
    total = None
    for place, weight in enumerate(weights):
        grads = own_ref if place < 3 else mate_ref
        part = grads[:, (place % 3) * size : (place % 3 + 1) * size]
        term = dot_f32(weight[pl.ds(start, rows), :], part, CONTRACT_LAST)
        total = term if total is None else total + term
    for fed in refs[6:-1]:
        total = total + fed[...].astype(jnp.float32)
    out_ref[...] = total.astype(out_ref.dtype)


def sum_kernel(own_ref, *refs):
    total = own_ref[...]
    for part in refs[:-1]:
        total = total + part[...].astype(jnp.float32)
    refs[-1][...] = total


def call(kernel, args, outs, fast_out=True, raw=False, sems=0):
    ints = [x.dtype == jnp.int32 for x in args]
    space = pltpu.HBM if raw else pltpu.VMEM
    args = [
        x if flag else pltpu.with_memory_space_constraint(x, space) for x, flag in zip(args, ints)
    ]
    there = pl.BlockSpec(memory_space=space)
    return pl.pallas_call(
        kernel,
        in_specs=[SMEM if flag else there for flag in ints],
        out_specs=[VMEM] * len(outs),
        out_shape=[
            pltpu.VMEM(shape, kind) if fast_out else jax.ShapeDtypeStruct(shape, kind)
            for shape, kind in outs
        ],
        scratch_shapes=[pltpu.SemaphoreType.DMA((sems,))] if sems else [],
        compiler_params=pltpu.CompilerParams(vmem_limit_bytes=16 << 20),
    )(*args)


def few_slabs(
    slabs,
    chips,
    grad_out,
    w_out,
    query_proj,
    key_proj,
    value_proj,
    w_query,
    w_key,
    w_value,
    tile_keys,
):
    rows, cols = grad_out.shape
    size = query_proj.shape[1]
    half, full = jnp.bfloat16, jnp.float32
    hops = sorted(range(1, chips), key=lambda step: (step & (step - 1) != 0, -step))

    def to_chip(x, step):
        return lax.ppermute(x, "tp", [(t, t ^ (2 * step)) for t in range(2 * chips)])

    def to_mate(x):
        return lax.ppermute(x, "tp", [(t, t ^ 1) for t in range(2 * chips)])

    def to_slab(x, turn):
        return lax.ppermute(x, "ctx", [(c, c ^ turn) for c in range(slabs)])

    blocks = [to_chip(grad_out, step) for step in range(1, chips)]
    (pack,) = call(
        pack_kernel, [query_proj, key_proj, value_proj], [((rows, 3 * size), half)],
        raw=True, sems=3,
    )
    packs = [pack] + [to_slab(pack, turn) for turn in range(1, slabs)]
    mate_out = to_mate(w_out)
    own_w = [w_query, w_key, w_value]
    mate_w = [to_mate(w) for w in own_w]
    near_out, near_grad = call(
        functools.partial(fetch_kernel, 2), [w_out, grad_out],
        [(w_out.shape, half), (grad_out.shape, half)], raw=True, sems=2,
    )
    prob_row, prob_col, attn_out = call(
        functools.partial(softmax_kernel, slabs, tile_keys.shape[1]),
        [tile_keys, *packs],
        [((rows, slabs * rows), full), ((slabs * rows, rows), full), ((slabs * rows, size), full)],
    )
    own_part, mate_part = call(
        functools.partial(attn_grad_kernel, chips, cols),
        [near_grad, *blocks, near_out, mate_out],
        [((rows, size), full), ((rows, size), full)],
    )
    grad = (own_part + to_mate(mate_part)).astype(half)
    grads = [grad] + [to_slab(grad, turn) for turn in range(1, slabs)]
    (d_query,) = call(
        functools.partial(query_grad_kernel, slabs),
        [grad, *packs, prob_row, attn_out],
        [((rows, size), half)],
    )
    (own_grads,) = call(
        functools.partial(key_grad_kernel, slabs),
        [*grads, *packs, d_query, prob_col, attn_out],
        [((rows, 3 * size), half)],
    )
    mate_grads = to_mate(own_grads)

    arrived = []
    for step in hops + [0]:
        (part,) = call(
            functools.partial(project_kernel, cols, step),
            [own_grads, mate_grads, *own_w, *mate_w],
            [((cols, rows), half if step else full)],
        )
        if step:
            arrived.append(to_chip(part, step))
    (out,) = call(sum_kernel, [part, *arrived], [((cols, rows), full)], fast_out=False)
    return out


def solution(mesh):
    slabs, shards = mesh.shape["ctx"], mesh.shape["tp"]
    chips = shards // 2
    few = slabs in (4, 8) and shards == 2 * chips and chips in (2, 4, 8)
    return jax.shard_map(
        functools.partial(few_slabs, slabs, chips) if few else many_slabs,
        mesh=mesh,
        in_specs=(
            P("ctx", "tp"),
            P("tp", None),
            P("ctx", "tp"),
            P("ctx", "tp"),
            P("ctx", "tp"),
            P(None, "tp"),
            P(None, "tp"),
            P(None, "tp"),
            P(),
        ),
        out_specs=P("tp", "ctx"),
        check_vma=False,
    )
```

```python
import functools

import jax
import jax.numpy as jnp
from jax import lax
from jax.experimental import pallas as pl
from jax.experimental.pallas import tpu as pltpu
from jax.sharding import PartitionSpec as P


TILE = 128
CONTRACT_LAST = (((1,), (1,)), ((), ()))
CONTRACT_FIRST = (((0,), (0,)), ((), ()))
VMEM = pl.BlockSpec(memory_space=pltpu.VMEM)
SMEM = pl.BlockSpec(memory_space=pltpu.SMEM)


def dot_f32(a, b, dims):
    return lax.dot_general(a, b, dims, preferred_element_type=jnp.float32)


def many_slabs(
    grad_out, w_out, query_proj, key_proj, value_proj, w_query, w_key, w_value, tile_keys
):
    row_count = query_proj.shape[0]
    head_size = query_proj.shape[1]
    score_scale = head_size ** (-0.5)
    tiles_here = row_count // TILE
    slab_index = lax.axis_index("ctx")
    d_attn = dot_f32(
        lax.all_gather(grad_out, "tp", axis=1, tiled=True), w_out, CONTRACT_LAST
    ).astype(jnp.bfloat16)
    keys_all, values_all = (
        lax.all_gather(key_proj, "ctx", axis=0, tiled=True),
        lax.all_gather(value_proj, "ctx", axis=0, tiled=True),
    )
    total_tiles = keys_all.shape[0] // TILE
    own_lists = lax.dynamic_slice_in_dim(tile_keys, slab_index * tiles_here, tiles_here, 0)
    all_tiles = jnp.arange(total_tiles, dtype=jnp.int32)
    tile_ok = jnp.any(own_lists[:, :, None] == all_tiles[None, None, :], axis=1)
    token_mask = jnp.repeat(jnp.repeat(tile_ok, TILE, axis=0), TILE, axis=1)
    scores = dot_f32(query_proj, keys_all, CONTRACT_LAST) * score_scale
    scores = jnp.where(token_mask, scores, -jnp.inf)
    row_max = jnp.max(scores, axis=1, keepdims=True)
    exponent = jnp.exp(scores - row_max)
    row_total = jnp.sum(exponent, axis=1, keepdims=True)
    prob_exact = exponent / row_total
    prob_half = prob_exact.astype(jnp.bfloat16)
    attn_out = jnp.dot(prob_half, values_all, preferred_element_type=jnp.float32)
    row_delta = jnp.sum(d_attn.astype(jnp.float32) * attn_out, axis=1, keepdims=True)
    d_prob = dot_f32(d_attn, values_all, CONTRACT_LAST)
    d_score = (prob_exact * (d_prob - row_delta) * score_scale).astype(jnp.bfloat16)
    d_query = jnp.dot(d_score, keys_all, preferred_element_type=jnp.float32).astype(jnp.bfloat16)
    key_part = dot_f32(d_score, query_proj, CONTRACT_FIRST)
    value_part = dot_f32(prob_half, d_attn, CONTRACT_FIRST)
    key_sums = lax.psum_scatter(
        jnp.concatenate([key_part, value_part], axis=1), "ctx", scatter_dimension=0, tiled=True
    )
    d_key = key_sums[:, :head_size].astype(jnp.bfloat16)
    d_value = key_sums[:, head_size:].astype(jnp.bfloat16)
    feature_sum = dot_f32(w_query, d_query, CONTRACT_LAST)
    feature_sum = feature_sum + dot_f32(w_key, d_key, CONTRACT_LAST)
    feature_sum = feature_sum + dot_f32(w_value, d_value, CONTRACT_LAST)
    return lax.psum_scatter(feature_sum, "tp", scatter_dimension=0, tiled=True)


def pack_kernel(query_ref, key_ref, value_ref, out_ref, sems):
    size = query_ref.shape[1]
    copies = [
        pltpu.make_async_copy(
            part, out_ref.at[:, place * size : (place + 1) * size], sems.at[place]
        )
        for place, part in enumerate((query_ref, key_ref, value_ref))
    ]
    for copy in copies:
        copy.start()
    for copy in copies:
        copy.wait()


def split_kernel(whole_ref, *refs):
    outs, sems = refs[:-1], refs[-1]
    copies, start = [], 0
    for place, out in enumerate(outs):
        span = pl.ds(start, out.shape[0])
        copies.append(pltpu.make_async_copy(whole_ref.at[span], out, sems.at[place]))
        start += out.shape[0]
    for copy in copies:
        copy.start()
    for copy in copies:
        copy.wait()


def attn_grad_kernel(cols, top, low, near, top2, low2, top3, low3, own_w, mate_w, own_ref, mate_ref):
    index = lax.axis_index("tp")
    blocks = [
        jnp.concatenate([top[...], low[...]], axis=0),
        near[...],
        jnp.concatenate([top2[...], low2[...]], axis=0),
        jnp.concatenate([top3[...], low3[...]], axis=0),
    ]
    own = jnp.zeros(own_ref.shape, jnp.float32)
    mate = jnp.zeros(own_ref.shape, jnp.float32)
    for step, block in enumerate(blocks):
        start = pl.multiple_of((index ^ (2 * step)) * cols, 128)
        own = own + dot_f32(block, own_w[:, pl.ds(start, cols)], CONTRACT_LAST)
        mate = mate + dot_f32(block, mate_w[:, pl.ds(start, cols)], CONTRACT_LAST)
    own_ref[...] = own
    mate_ref[...] = mate


def softmax_kernel(slabs, keep, lists_ref, *refs):
    packs = refs[:slabs]
    row_ref, col_ref, attn_ref = refs[slabs:]
    rows = packs[0].shape[0]
    size = packs[0].shape[1] // 3
    tiles = rows // TILE
    slab = lax.axis_index("ctx")
    scale = size ** (-0.5)
    keys = jnp.concatenate([pack[:, size : 2 * size] for pack in packs], axis=0)
    values = jnp.concatenate([pack[:, 2 * size :] for pack in packs], axis=0)
    for turn in range(slabs):
        for tile in range(tiles):
            query_tile = (slab ^ turn) * tiles + tile
            span = pl.ds(turn * rows + tile * TILE, TILE)
            scores = dot_f32(packs[turn][pl.ds(tile * TILE, TILE), :size], keys, CONTRACT_LAST)
            scores = scores * scale
            parts = []
            for other in range(slabs * tiles):
                key_tile = (slab ^ (other // tiles)) * tiles + other % tiles
                listed = lists_ref[query_tile, 0] == key_tile
                for place in range(1, keep):
                    listed = listed | (lists_ref[query_tile, place] == key_tile)
                part = scores[:, other * TILE : (other + 1) * TILE]
                parts.append(jnp.where(listed, part, -jnp.inf))
            scores = jnp.concatenate(parts, axis=1)
            exponent = jnp.exp(scores - jnp.max(scores, axis=1, keepdims=True))
            prob = exponent / jnp.sum(exponent, axis=1, keepdims=True)
            attn_ref[span, :] = jnp.dot(
                prob.astype(jnp.bfloat16), values, preferred_element_type=jnp.float32
            )
            col_ref[span, :] = prob[:, :rows]
            if turn == 0:
                row_ref[pl.ds(tile * TILE, TILE), :] = prob


def query_grad_kernel(slabs, grad_ref, *refs):
    packs = refs[:slabs]
    row_ref, attn_ref, out_ref = refs[slabs:]
    rows = packs[0].shape[0]
    size = packs[0].shape[1] // 3
    scale = size ** (-0.5)
    grad = grad_ref[...]
    keys = jnp.concatenate([pack[:, size : 2 * size] for pack in packs], axis=0)
    values = jnp.concatenate([pack[:, 2 * size :] for pack in packs], axis=0)
    delta = jnp.sum(grad.astype(jnp.float32) * attn_ref[:rows, :], axis=1, keepdims=True)
    d_prob = dot_f32(grad, values, CONTRACT_LAST)
    d_score = (row_ref[...] * (d_prob - delta) * scale).astype(jnp.bfloat16)
    out_ref[...] = jnp.dot(d_score, keys, preferred_element_type=jnp.float32).astype(jnp.bfloat16)


def key_grad_kernel(slabs, *refs):
    grads = refs[:slabs]
    packs = refs[slabs : 2 * slabs]
    query_ref, col_ref, attn_ref, out_ref = refs[2 * slabs :]
    size = packs[0].shape[1] // 3
    scale = size ** (-0.5)
    queries = jnp.concatenate([pack[:, :size] for pack in packs], axis=0)
    grad = jnp.concatenate([part[...] for part in grads], axis=0)
    prob = col_ref[...]
    delta = jnp.sum(grad.astype(jnp.float32) * attn_ref[...], axis=1, keepdims=True)
    d_prob = dot_f32(grad, packs[0][:, 2 * size :], CONTRACT_LAST)
    d_score = (prob * (d_prob - delta) * scale).astype(jnp.bfloat16)
    out_ref[:, :size] = query_ref[...]
    out_ref[:, size : 2 * size] = dot_f32(d_score, queries, CONTRACT_FIRST).astype(jnp.bfloat16)
    out_ref[:, 2 * size :] = dot_f32(prob.astype(jnp.bfloat16), grad, CONTRACT_FIRST).astype(
        jnp.bfloat16
    )


def project_kernel(block, step, first, own_ref, mate_ref, *refs):
    weights, out_ref = refs[:6], refs[-1]
    rows = out_ref.shape[0]
    start = pl.multiple_of((lax.axis_index("tp") ^ (2 * step)) * block + first, 16)
    size = own_ref.shape[1] // 3
    total = None
    for place, weight in enumerate(weights):
        grads = own_ref if place < 3 else mate_ref
        part = grads[:, (place % 3) * size : (place % 3 + 1) * size]
        term = dot_f32(weight[pl.ds(start, rows), :], part, CONTRACT_LAST)
        total = term if total is None else total + term
    for fed in refs[6:-1]:
        total = total + fed[...].astype(jnp.float32)
    out_ref[...] = total.astype(out_ref.dtype)


def sum_kernel(own_ref, near, top2, low2, low3, out_ref):
    full = jnp.float32
    cut = top2.shape[0]
    out_ref[:cut, :] = own_ref[:cut, :] + near[:cut, :].astype(full) + top2[...].astype(full)
    low = low2[...].astype(full) + low3[...].astype(full)
    out_ref[cut:, :] = own_ref[cut:, :] + near[cut:, :].astype(full) + low


def call(kernel, args, outs, fast_out=True, raw=False, sems=0):
    ints = [x.dtype == jnp.int32 for x in args]
    space = pltpu.HBM if raw else pltpu.VMEM
    args = [
        x if flag else pltpu.with_memory_space_constraint(x, space) for x, flag in zip(args, ints)
    ]
    there = pl.BlockSpec(memory_space=space)
    return pl.pallas_call(
        kernel,
        in_specs=[SMEM if flag else there for flag in ints],
        out_specs=[VMEM] * len(outs),
        out_shape=[
            pltpu.VMEM(shape, kind) if fast_out else jax.ShapeDtypeStruct(shape, kind)
            for shape, kind in outs
        ],
        scratch_shapes=[pltpu.SemaphoreType.DMA((sems,))] if sems else [],
        compiler_params=pltpu.CompilerParams(vmem_limit_bytes=16 << 20),
    )(*args)


def few_slabs(
    slabs,
    grad_out,
    w_out,
    query_proj,
    key_proj,
    value_proj,
    w_query,
    w_key,
    w_value,
    tile_keys,
):
    rows, cols = grad_out.shape
    size = query_proj.shape[1]
    half, full = jnp.bfloat16, jnp.float32
    cut, feature_cut = rows // 2, cols // 2

    def to_chip(x, step):
        return lax.ppermute(x, "tp", [(t, t ^ (2 * step)) for t in range(8)])

    def to_mate(x):
        return lax.ppermute(x, "tp", [(t, t ^ 1) for t in range(8)])

    def to_slab(x, turn):
        return lax.ppermute(x, "ctx", [(c, c ^ turn) for c in range(slabs)])

    top, low = call(
        split_kernel, [grad_out], [((cut, cols), half), ((rows - cut, cols), half)],
        raw=True, sems=2,
    )
    top2 = to_chip(top, 2)
    near = to_chip(grad_out, 1)
    low2 = to_chip(low, 2)
    low3 = to_chip(low, 3)
    top3 = to_chip(top2, 1)
    (pack,) = call(
        pack_kernel, [query_proj, key_proj, value_proj], [((rows, 3 * size), half)],
        raw=True, sems=3,
    )
    packs = [pack] + [to_slab(pack, turn) for turn in range(1, slabs)]
    mate_out = to_mate(w_out)
    own_w = [w_query, w_key, w_value]
    mate_w = [to_mate(w) for w in own_w]
    (near_out,) = call(split_kernel, [w_out], [(w_out.shape, half)], raw=True, sems=1)
    prob_row, prob_col, attn_out = call(
        functools.partial(softmax_kernel, slabs, tile_keys.shape[1]),
        [tile_keys, *packs],
        [((rows, slabs * rows), full), ((slabs * rows, rows), full), ((slabs * rows, size), full)],
    )
    own_part, mate_part = call(
        functools.partial(attn_grad_kernel, cols),
        [top, low, near, top2, low2, top3, low3, near_out, mate_out],
        [((rows, size), full), ((rows, size), full)],
    )
    grad = (own_part + to_mate(mate_part)).astype(half)
    grads = [grad] + [to_slab(grad, turn) for turn in range(1, slabs)]
    (d_query,) = call(
        functools.partial(query_grad_kernel, slabs),
        [grad, *packs, prob_row, attn_out],
        [((rows, size), half)],
    )
    (own_grads,) = call(
        functools.partial(key_grad_kernel, slabs),
        [*grads, *packs, d_query, prob_col, attn_out],
        [((rows, 3 * size), half)],
    )
    mate_grads = to_mate(own_grads)


    def project(step, first, count, kind, *fed):
        (part,) = call(
            functools.partial(project_kernel, cols, step, first),
            [own_grads, mate_grads, *own_w, *mate_w, *fed],
            [((count, rows), kind)],
        )
        return part

    rest = cols - feature_cut
    fed = to_chip(project(3, 0, feature_cut, half), 1)
    low3 = to_chip(project(3, feature_cut, rest, half), 3)
    low2 = to_chip(project(2, feature_cut, rest, half), 2)
    near = to_chip(project(1, 0, cols, half), 1)
    top2 = to_chip(project(2, 0, feature_cut, half, fed), 2)
    (out,) = call(
        sum_kernel,
        [project(0, 0, cols, full), near, top2, low2, low3],
        [((cols, rows), full)],
        fast_out=False,
    )
    return out


def solution(mesh):
    slabs, shards = mesh.shape["ctx"], mesh.shape["tp"]
    few = slabs in (4, 8) and shards == 8
    return jax.shard_map(
        functools.partial(few_slabs, slabs) if few else many_slabs,
        mesh=mesh,
        in_specs=(
            P("ctx", "tp"),
            P("tp", None),
            P("ctx", "tp"),
            P("ctx", "tp"),
            P("ctx", "tp"),
            P(None, "tp"),
            P(None, "tp"),
            P(None, "tp"),
            P(),
        ),
        out_specs=P("tp", "ctx"),
        check_vma=False,
    )
```

```python
import functools

import jax
import jax.numpy as jnp
from jax import lax
from jax.experimental import pallas as pl
from jax.experimental.pallas import tpu as pltpu
from jax.sharding import PartitionSpec as P


TILE = 128
CONTRACT_LAST = (((1,), (1,)), ((), ()))
CONTRACT_FIRST = (((0,), (0,)), ((), ()))
VMEM = pl.BlockSpec(memory_space=pltpu.VMEM)
SMEM = pl.BlockSpec(memory_space=pltpu.SMEM)


def dot_f32(a, b, dims):
    return lax.dot_general(a, b, dims, preferred_element_type=jnp.float32)


def many_slabs(
    grad_out, w_out, query_proj, key_proj, value_proj, w_query, w_key, w_value, tile_keys
):
    row_count = query_proj.shape[0]
    head_size = query_proj.shape[1]
    score_scale = head_size ** (-0.5)
    tiles_here = row_count // TILE
    slab_index = lax.axis_index("ctx")
    d_attn = dot_f32(
        lax.all_gather(grad_out, "tp", axis=1, tiled=True), w_out, CONTRACT_LAST
    ).astype(jnp.bfloat16)
    keys_all, values_all = (
        lax.all_gather(key_proj, "ctx", axis=0, tiled=True),
        lax.all_gather(value_proj, "ctx", axis=0, tiled=True),
    )
    total_tiles = keys_all.shape[0] // TILE
    own_lists = lax.dynamic_slice_in_dim(tile_keys, slab_index * tiles_here, tiles_here, 0)
    all_tiles = jnp.arange(total_tiles, dtype=jnp.int32)
    tile_ok = jnp.any(own_lists[:, :, None] == all_tiles[None, None, :], axis=1)
    token_mask = jnp.repeat(jnp.repeat(tile_ok, TILE, axis=0), TILE, axis=1)
    scores = dot_f32(query_proj, keys_all, CONTRACT_LAST) * score_scale
    scores = jnp.where(token_mask, scores, -jnp.inf)
    row_max = jnp.max(scores, axis=1, keepdims=True)
    exponent = jnp.exp(scores - row_max)
    row_total = jnp.sum(exponent, axis=1, keepdims=True)
    prob_exact = exponent / row_total
    prob_half = prob_exact.astype(jnp.bfloat16)
    attn_out = jnp.dot(prob_half, values_all, preferred_element_type=jnp.float32)
    row_delta = jnp.sum(d_attn.astype(jnp.float32) * attn_out, axis=1, keepdims=True)
    d_prob = dot_f32(d_attn, values_all, CONTRACT_LAST)
    d_score = (prob_exact * (d_prob - row_delta) * score_scale).astype(jnp.bfloat16)
    d_query = jnp.dot(d_score, keys_all, preferred_element_type=jnp.float32).astype(jnp.bfloat16)
    key_part = dot_f32(d_score, query_proj, CONTRACT_FIRST)
    value_part = dot_f32(prob_half, d_attn, CONTRACT_FIRST)
    key_sums = lax.psum_scatter(
        jnp.concatenate([key_part, value_part], axis=1), "ctx", scatter_dimension=0, tiled=True
    )
    d_key = key_sums[:, :head_size].astype(jnp.bfloat16)
    d_value = key_sums[:, head_size:].astype(jnp.bfloat16)
    feature_sum = dot_f32(w_query, d_query, CONTRACT_LAST)
    feature_sum = feature_sum + dot_f32(w_key, d_key, CONTRACT_LAST)
    feature_sum = feature_sum + dot_f32(w_value, d_value, CONTRACT_LAST)
    return lax.psum_scatter(feature_sum, "tp", scatter_dimension=0, tiled=True)


def pack_kernel(query_ref, key_ref, value_ref, w_ref, out_ref, w_out_ref, sems):
    size = query_ref.shape[1]
    copies = [
        pltpu.make_async_copy(
            part, out_ref.at[:, place * size : (place + 1) * size], sems.at[place]
        )
        for place, part in enumerate((query_ref, key_ref, value_ref))
    ]
    copies.append(pltpu.make_async_copy(w_ref, w_out_ref, sems.at[3]))
    for copy in copies:
        copy.start()
    for copy in copies:
        copy.wait()


def split_kernel(whole_ref, *refs):
    outs, sems = refs[:-1], refs[-1]
    copies, start = [], 0
    for place, out in enumerate(outs):
        span = pl.ds(start, out.shape[0])
        copies.append(pltpu.make_async_copy(whole_ref.at[span], out, sems.at[place]))
        start += out.shape[0]
    for copy in copies:
        copy.start()
    for copy in copies:
        copy.wait()


def attn_grad_kernel(cols, top, low, near, top2, low2, top3, low3, own_w, mate_w, out_ref):
    index = lax.axis_index("tp")
    blocks = [
        jnp.concatenate([top[...], low[...]], axis=0),
        near[...],
        jnp.concatenate([top2[...], low2[...]], axis=0),
        jnp.concatenate([top3[...], low3[...]], axis=0),
    ]
    total = None
    for step, block in enumerate(blocks):
        start = pl.multiple_of((index ^ (2 * step)) * cols, 128)
        weight = jnp.concatenate(
            [own_w[:, pl.ds(start, cols)], mate_w[:, pl.ds(start, cols)]], axis=0
        )
        term = dot_f32(block, weight, CONTRACT_LAST)
        total = term if total is None else total + term
    out_ref[...] = total


def merge_kernel(own_ref, mate_ref, out_ref, own_out_ref):
    size = own_out_ref.shape[1]
    own = (own_ref[:, :size] + mate_ref[:, size:]).astype(jnp.bfloat16)
    out_ref[:, :size] = own
    out_ref[:, size:] = (own_ref[:, size:] + mate_ref[:, :size]).astype(jnp.bfloat16)
    own_out_ref[...] = own


def softmax_kernel(slabs, keep, lists_ref, *refs):
    packs = refs[:slabs]
    row_ref, col_ref, attn_ref = refs[slabs:]
    rows = packs[0].shape[0]
    size = packs[0].shape[1] // 3
    tiles = rows // TILE
    slab = lax.axis_index("ctx")
    scale = size ** (-0.5)
    keys = jnp.concatenate([pack[:, size : 2 * size] for pack in packs], axis=0)
    values = jnp.concatenate([pack[:, 2 * size :] for pack in packs], axis=0)
    for turn in range(slabs):
        for tile in range(tiles):
            query_tile = (slab ^ turn) * tiles + tile
            span = pl.ds(turn * rows + tile * TILE, TILE)
            scores = dot_f32(packs[turn][pl.ds(tile * TILE, TILE), :size], keys, CONTRACT_LAST)
            scores = scores * scale
            parts = []
            for other in range(slabs * tiles):
                key_tile = (slab ^ (other // tiles)) * tiles + other % tiles
                listed = lists_ref[query_tile, 0] == key_tile
                for place in range(1, keep):
                    listed = listed | (lists_ref[query_tile, place] == key_tile)
                part = scores[:, other * TILE : (other + 1) * TILE]
                parts.append(jnp.where(listed, part, -jnp.inf))
            scores = jnp.concatenate(parts, axis=1)
            exponent = jnp.exp(scores - jnp.max(scores, axis=1, keepdims=True))
            prob = exponent * (1.0 / jnp.sum(exponent, axis=1, keepdims=True))
            attn_ref[span, :] = jnp.dot(
                prob.astype(jnp.bfloat16), values, preferred_element_type=jnp.float32
            )
            col_ref[span, :] = prob[:, :rows]
            if turn == 0:
                row_ref[pl.ds(tile * TILE, TILE), :] = prob


def query_grad_kernel(slabs, grad_ref, *refs):
    packs = refs[:slabs]
    row_ref, attn_ref, out_ref = refs[slabs:]
    rows = packs[0].shape[0]
    size = packs[0].shape[1] // 3
    scale = size ** (-0.5)
    grad = grad_ref[...]
    keys = jnp.concatenate([pack[:, size : 2 * size] for pack in packs], axis=0)
    values = jnp.concatenate([pack[:, 2 * size :] for pack in packs], axis=0)
    delta = jnp.sum(grad.astype(jnp.float32) * attn_ref[:rows, :], axis=1, keepdims=True)
    d_prob = dot_f32(grad, values, CONTRACT_LAST)
    d_score = (row_ref[...] * (d_prob - delta) * scale).astype(jnp.bfloat16)
    out_ref[...] = jnp.dot(d_score, keys, preferred_element_type=jnp.float32).astype(jnp.bfloat16)


def key_grad_kernel(slabs, own, beside, swapped, across, *refs):
    packs = refs[:slabs]
    query_ref, col_ref, attn_ref, out_ref = refs[slabs:]
    size = packs[0].shape[1] // 3
    scale = size ** (-0.5)
    even = (lax.axis_index("tp") & 1) == 0
    near, far = beside[:, :size], swapped[:, size:]
    first, second = jnp.where(even, near, far), jnp.where(even, far, near)
    queries = jnp.concatenate([pack[:, :size] for pack in packs], axis=0)
    grad = jnp.concatenate([own[...], first, second, across[...]], axis=0)
    prob = col_ref[...]
    delta = jnp.sum(grad.astype(jnp.float32) * attn_ref[...], axis=1, keepdims=True)
    d_prob = dot_f32(grad, packs[0][:, 2 * size :], CONTRACT_LAST)
    d_score = (prob * (d_prob - delta) * scale).astype(jnp.bfloat16)
    out_ref[:, :size] = query_ref[...]
    out_ref[:, size : 2 * size] = dot_f32(d_score, queries, CONTRACT_FIRST).astype(jnp.bfloat16)
    out_ref[:, 2 * size :] = dot_f32(prob.astype(jnp.bfloat16), grad, CONTRACT_FIRST).astype(
        jnp.bfloat16
    )


def project_kernel(block, step, first, own_ref, mate_ref, *refs):
    weights, out_ref = refs[:6], refs[-1]
    rows = out_ref.shape[0]
    start = pl.multiple_of((lax.axis_index("tp") ^ (2 * step)) * block + first, 16)
    size = own_ref.shape[1] // 3
    total = None
    for place, weight in enumerate(weights):
        grads = own_ref if place < 3 else mate_ref
        part = grads[:, (place % 3) * size : (place % 3 + 1) * size]
        term = dot_f32(weight[pl.ds(start, rows), :], part, CONTRACT_LAST)
        total = term if total is None else total + term
    for fed in refs[6:-1]:
        total = total + fed[...].astype(jnp.float32)
    out_ref[...] = total.astype(out_ref.dtype)


def sum_kernel(own_ref, near, top2, low2, low3, out_ref):
    full = jnp.float32
    cut = top2.shape[0]
    out_ref[:cut, :] = own_ref[:cut, :] + near[:cut, :].astype(full) + top2[...].astype(full)
    low = low2[...].astype(full) + low3[...].astype(full)
    out_ref[cut:, :] = own_ref[cut:, :] + near[cut:, :].astype(full) + low


def call(kernel, args, outs, fast_out=True, raw=False, sems=0):
    ints = [x.dtype == jnp.int32 for x in args]
    space = pltpu.HBM if raw else pltpu.VMEM
    args = [
        x if flag else pltpu.with_memory_space_constraint(x, space) for x, flag in zip(args, ints)
    ]
    there = pl.BlockSpec(memory_space=space)
    return pl.pallas_call(
        kernel,
        in_specs=[SMEM if flag else there for flag in ints],
        out_specs=[VMEM] * len(outs),
        out_shape=[
            pltpu.VMEM(shape, kind) if fast_out else jax.ShapeDtypeStruct(shape, kind)
            for shape, kind in outs
        ],
        scratch_shapes=[pltpu.SemaphoreType.DMA((sems,))] if sems else [],
        compiler_params=pltpu.CompilerParams(vmem_limit_bytes=16 << 20),
    )(*args)


def few_slabs(
    slabs,
    grad_out,
    w_out,
    query_proj,
    key_proj,
    value_proj,
    w_query,
    w_key,
    w_value,
    tile_keys,
):
    rows, cols = grad_out.shape
    size = query_proj.shape[1]
    half, full = jnp.bfloat16, jnp.float32
    cut, feature_cut = rows // 2, cols * 3 // 5 // 16 * 16

    def to_chip(x, step):
        return lax.ppermute(x, "tp", [(t, t ^ (2 * step)) for t in range(8)])

    def to_mate(x):
        return lax.ppermute(x, "tp", [(t, t ^ 1) for t in range(8)])

    def to_slab(x, turn):
        return lax.ppermute(x, "ctx", [(c, c ^ turn) for c in range(slabs)])

    def to_beside(x):
        pairs = [(c * 8 + t, (c ^ (1 + t % 2)) * 8 + t) for c in range(slabs) for t in range(8)]
        return lax.ppermute(x, ("ctx", "tp"), pairs)

    top, low = call(
        split_kernel, [grad_out], [((cut, cols), half), ((rows - cut, cols), half)],
        raw=True, sems=2,
    )
    top2 = to_chip(top, 2)
    near = to_chip(grad_out, 1)
    low2 = to_chip(low, 2)
    low3 = to_chip(low, 3)
    top3 = to_chip(top2, 1)
    pack, near_out = call(
        pack_kernel, [query_proj, key_proj, value_proj, w_out],
        [((rows, 3 * size), half), (w_out.shape, half)], raw=True, sems=4,
    )
    packs = [pack] + [to_slab(pack, turn) for turn in range(1, slabs)]
    mate_out = to_mate(w_out)
    own_w = [w_query, w_key, w_value]
    mate_w = [to_mate(w) for w in own_w]
    prob_row, prob_col, attn_out = call(
        functools.partial(softmax_kernel, slabs, tile_keys.shape[1]),
        [tile_keys, *packs],
        [((rows, slabs * rows), full), ((slabs * rows, rows), full), ((slabs * rows, size), full)],
    )
    (part,) = call(
        functools.partial(attn_grad_kernel, cols),
        [top, low, near, top2, low2, top3, low3, near_out, mate_out],
        [((rows, 2 * size), full)],
    )
    both, grad = call(
        merge_kernel, [part, to_mate(part)],
        [((rows, 2 * size), half), ((rows, size), half)],
    )
    beside = to_beside(both)
    across = to_slab(grad, 3)
    swapped = to_mate(beside)
    (d_query,) = call(
        functools.partial(query_grad_kernel, slabs),
        [grad, *packs, prob_row, attn_out],
        [((rows, size), half)],
    )
    (own_grads,) = call(
        functools.partial(key_grad_kernel, slabs),
        [grad, beside, swapped, across, *packs, d_query, prob_col, attn_out],
        [((rows, 3 * size), half)],
    )
    mate_grads = to_mate(own_grads)


    def project(step, first, count, kind, *fed):
        (part,) = call(
            functools.partial(project_kernel, cols, step, first),
            [own_grads, mate_grads, *own_w, *mate_w, *fed],
            [((count, rows), kind)],
        )
        return part

    rest = cols - feature_cut
    fed = to_chip(project(3, 0, feature_cut, half), 1)
    low3 = to_chip(project(3, feature_cut, rest, half), 3)
    low2 = to_chip(project(2, feature_cut, rest, half), 2)
    near = to_chip(project(1, 0, cols, half), 1)
    top2 = to_chip(project(2, 0, feature_cut, half, fed), 2)
    (out,) = call(
        sum_kernel,
        [project(0, 0, cols, full), near, top2, low2, low3],
        [((cols, rows), full)],
        fast_out=False,
    )
    return out


def solution(mesh):
    slabs, shards = mesh.shape["ctx"], mesh.shape["tp"]
    few = slabs == 4 and shards == 8
    return jax.shard_map(
        functools.partial(few_slabs, slabs) if few else many_slabs,
        mesh=mesh,
        in_specs=(
            P("ctx", "tp"),
            P("tp", None),
            P("ctx", "tp"),
            P("ctx", "tp"),
            P("ctx", "tp"),
            P(None, "tp"),
            P(None, "tp"),
            P(None, "tp"),
            P(),
        ),
        out_specs=P("tp", "ctx"),
        check_vma=False,
    )
```

```python
import functools

import jax
import jax.numpy as jnp
from jax import lax
from jax.experimental import pallas as pl
from jax.experimental.pallas import tpu as pltpu
from jax.sharding import PartitionSpec as P


TILE = 128
EARLY = (0, 1, 2)
CONTRACT_LAST = (((1,), (1,)), ((), ()))
CONTRACT_FIRST = (((0,), (0,)), ((), ()))
VMEM = pl.BlockSpec(memory_space=pltpu.VMEM)
SMEM = pl.BlockSpec(memory_space=pltpu.SMEM)


def dot_f32(a, b, dims):
    return lax.dot_general(a, b, dims, preferred_element_type=jnp.float32)


def many_slabs(
    grad_out, w_out, query_proj, key_proj, value_proj, w_query, w_key, w_value, tile_keys
):
    row_count = query_proj.shape[0]
    head_size = query_proj.shape[1]
    score_scale = head_size ** (-0.5)
    tiles_here = row_count // TILE
    slab_index = lax.axis_index("ctx")
    d_attn = dot_f32(
        lax.all_gather(grad_out, "tp", axis=1, tiled=True), w_out, CONTRACT_LAST
    ).astype(jnp.bfloat16)
    keys_all, values_all = (
        lax.all_gather(key_proj, "ctx", axis=0, tiled=True),
        lax.all_gather(value_proj, "ctx", axis=0, tiled=True),
    )
    total_tiles = keys_all.shape[0] // TILE
    own_lists = lax.dynamic_slice_in_dim(tile_keys, slab_index * tiles_here, tiles_here, 0)
    all_tiles = jnp.arange(total_tiles, dtype=jnp.int32)
    tile_ok = jnp.any(own_lists[:, :, None] == all_tiles[None, None, :], axis=1)
    token_mask = jnp.repeat(jnp.repeat(tile_ok, TILE, axis=0), TILE, axis=1)
    scores = dot_f32(query_proj, keys_all, CONTRACT_LAST) * score_scale
    scores = jnp.where(token_mask, scores, -jnp.inf)
    row_max = jnp.max(scores, axis=1, keepdims=True)
    exponent = jnp.exp(scores - row_max)
    row_total = jnp.sum(exponent, axis=1, keepdims=True)
    prob_exact = exponent / row_total
    prob_half = prob_exact.astype(jnp.bfloat16)
    attn_out = jnp.dot(prob_half, values_all, preferred_element_type=jnp.float32)
    row_delta = jnp.sum(d_attn.astype(jnp.float32) * attn_out, axis=1, keepdims=True)
    d_prob = dot_f32(d_attn, values_all, CONTRACT_LAST)
    d_score = (prob_exact * (d_prob - row_delta) * score_scale).astype(jnp.bfloat16)
    d_query = jnp.dot(d_score, keys_all, preferred_element_type=jnp.float32).astype(jnp.bfloat16)
    key_part = dot_f32(d_score, query_proj, CONTRACT_FIRST)
    value_part = dot_f32(prob_half, d_attn, CONTRACT_FIRST)
    key_sums = lax.psum_scatter(
        jnp.concatenate([key_part, value_part], axis=1), "ctx", scatter_dimension=0, tiled=True
    )
    d_key = key_sums[:, :head_size].astype(jnp.bfloat16)
    d_value = key_sums[:, head_size:].astype(jnp.bfloat16)
    feature_sum = dot_f32(w_query, d_query, CONTRACT_LAST)
    feature_sum = feature_sum + dot_f32(w_key, d_key, CONTRACT_LAST)
    feature_sum = feature_sum + dot_f32(w_value, d_value, CONTRACT_LAST)
    return lax.psum_scatter(feature_sum, "tp", scatter_dimension=0, tiled=True)


def pack_kernel(query_ref, key_ref, value_ref, w_ref, out_ref, w_out_ref, sems):
    size = query_ref.shape[1]
    copies = [
        pltpu.make_async_copy(
            part, out_ref.at[:, place * size : (place + 1) * size], sems.at[place]
        )
        for place, part in enumerate((query_ref, key_ref, value_ref))
    ]
    cols = w_out_ref.shape[1] // 4
    for step in range(4):
        start = pl.multiple_of((lax.axis_index("tp") ^ (2 * step)) * cols, 128)
        copies.append(
            pltpu.make_async_copy(
                w_ref.at[:, pl.ds(start, cols)],
                w_out_ref.at[:, step * cols : (step + 1) * cols],
                sems.at[3 + step],
            )
        )
    for copy in copies:
        copy.start()
    for copy in copies:
        copy.wait()


def split_kernel(whole_ref, *refs):
    outs, sems = refs[:-1], refs[-1]
    copies, start = [], 0
    for place, out in enumerate(outs):
        span = pl.ds(start, out.shape[0])
        copies.append(pltpu.make_async_copy(whole_ref.at[span], out, sems.at[place]))
        start += out.shape[0]
    for copy in copies:
        copy.start()
    for copy in copies:
        copy.wait()


def attn_grad_kernel(cols, steps, *refs):
    index = lax.axis_index("tp")
    count = sum(1 if step == 1 else 2 for step in steps)
    parts, own_w, mate_w, out_ref = list(refs[:count]), refs[count], refs[count + 1], refs[-1]
    total = refs[-2][...] if len(refs) > count + 3 else None
    for step in steps:
        start = pl.multiple_of((index ^ (2 * step)) * cols, 128)
        weight = jnp.concatenate(
            [own_w[:, step * cols : (step + 1) * cols], mate_w[:, pl.ds(start, cols)]], axis=0
        )
        pieces = [parts.pop(0)[...] for _ in range(1 if step == 1 else 2)]
        block = jnp.concatenate(pieces, axis=0)
        term = dot_f32(block, weight, CONTRACT_LAST)
        total = term if total is None else total + term
    out_ref[...] = total


def merge_kernel(own_ref, mate_ref, out_ref, own_out_ref):
    size = own_out_ref.shape[1]
    own = (own_ref[:, :size] + mate_ref[:, size:]).astype(jnp.bfloat16)
    out_ref[:, :size] = own
    out_ref[:, size:] = (own_ref[:, size:] + mate_ref[:, :size]).astype(jnp.bfloat16)
    own_out_ref[...] = own


def softmax_kernel(slabs, keep, lists_ref, *refs):
    packs = refs[:slabs]
    row_ref, col_ref, attn_ref = refs[slabs:]
    rows = packs[0].shape[0]
    size = packs[0].shape[1] // 3
    tiles = rows // TILE
    slab = lax.axis_index("ctx")
    scale = size ** (-0.5)
    keys = jnp.concatenate([pack[:, size : 2 * size] for pack in packs], axis=0)
    values = jnp.concatenate([pack[:, 2 * size :] for pack in packs], axis=0)
    for turn in range(slabs):
        for tile in range(tiles):
            query_tile = (slab ^ turn) * tiles + tile
            span = pl.ds(turn * rows + tile * TILE, TILE)
            scores = dot_f32(packs[turn][pl.ds(tile * TILE, TILE), :size], keys, CONTRACT_LAST)
            scores = scores * scale
            parts = []
            for other in range(slabs * tiles):
                key_tile = (slab ^ (other // tiles)) * tiles + other % tiles
                listed = lists_ref[query_tile, 0] == key_tile
                for place in range(1, keep):
                    listed = listed | (lists_ref[query_tile, place] == key_tile)
                part = scores[:, other * TILE : (other + 1) * TILE]
                parts.append(jnp.where(listed, part, -jnp.inf))
            scores = jnp.concatenate(parts, axis=1)
            exponent = jnp.exp(scores - jnp.max(scores, axis=1, keepdims=True))
            prob = exponent * (1.0 / jnp.sum(exponent, axis=1, keepdims=True))
            attn_ref[span, :] = jnp.dot(
                prob.astype(jnp.bfloat16), values, preferred_element_type=jnp.float32
            )
            col_ref[span, :] = prob[:, :rows]
            if turn == 0:
                row_ref[pl.ds(tile * TILE, TILE), :] = prob


def query_grad_kernel(slabs, grad_ref, *refs):
    packs = refs[:slabs]
    row_ref, attn_ref, out_ref = refs[slabs:]
    rows = packs[0].shape[0]
    size = packs[0].shape[1] // 3
    scale = size ** (-0.5)
    grad = grad_ref[...]
    keys = jnp.concatenate([pack[:, size : 2 * size] for pack in packs], axis=0)
    values = jnp.concatenate([pack[:, 2 * size :] for pack in packs], axis=0)
    delta = jnp.sum(grad.astype(jnp.float32) * attn_ref[:rows, :], axis=1, keepdims=True)
    d_prob = dot_f32(grad, values, CONTRACT_LAST)
    d_score = (row_ref[...] * (d_prob - delta) * scale).astype(jnp.bfloat16)
    out_ref[...] = jnp.dot(d_score, keys, preferred_element_type=jnp.float32).astype(jnp.bfloat16)


def key_grad_kernel(slabs, own, beside, swapped, across, *refs):
    packs = refs[:slabs]
    query_ref, col_ref, attn_ref, out_ref = refs[slabs:]
    size = packs[0].shape[1] // 3
    scale = size ** (-0.5)
    even = (lax.axis_index("tp") & 1) == 0
    near, far = beside[:, :size], swapped[:, size:]
    first, second = jnp.where(even, near, far), jnp.where(even, far, near)
    queries = jnp.concatenate([pack[:, :size] for pack in packs], axis=0)
    grad = jnp.concatenate([own[...], first, second, across[...]], axis=0)
    prob = col_ref[...]
    delta = jnp.sum(grad.astype(jnp.float32) * attn_ref[...], axis=1, keepdims=True)
    d_prob = dot_f32(grad, packs[0][:, 2 * size :], CONTRACT_LAST)
    d_score = (prob * (d_prob - delta) * scale).astype(jnp.bfloat16)
    out_ref[:, :size] = query_ref[...]
    out_ref[:, size : 2 * size] = dot_f32(d_score, queries, CONTRACT_FIRST).astype(jnp.bfloat16)
    out_ref[:, 2 * size :] = dot_f32(prob.astype(jnp.bfloat16), grad, CONTRACT_FIRST).astype(
        jnp.bfloat16
    )


def project_own_kernel(block, own_ref, *refs):
    weights, out_ref = refs[:3], refs[3]
    size = own_ref.shape[1] // 3
    for step in range(out_ref.shape[0] // block):
        start = pl.multiple_of((lax.axis_index("tp") ^ (2 * step)) * block, 16)
        total = None
        for place, weight in enumerate(weights):
            part = own_ref[:, place * size : (place + 1) * size]
            term = dot_f32(weight[pl.ds(start, block), :], part, CONTRACT_LAST)
            total = term if total is None else total + term
        out_ref[step * block : (step + 1) * block, :] = total


def project_kernel(block, step, first, own_ref, mate_ref, *refs):
    weights, out_ref = refs[:3], refs[-1]
    rows = out_ref.shape[0]
    start = pl.multiple_of((lax.axis_index("tp") ^ (2 * step)) * block + first, 16)
    size = mate_ref.shape[1] // 3
    total = own_ref[step * block + first : step * block + first + rows, :]
    for place, weight in enumerate(weights):
        part = mate_ref[:, place * size : (place + 1) * size]
        total = total + dot_f32(weight[pl.ds(start, rows), :], part, CONTRACT_LAST)
    for fed in refs[3:-1]:
        total = total + fed[...].astype(jnp.float32)
    out_ref[...] = total.astype(out_ref.dtype)


def sum_kernel(own_ref, near, top2, low2, low3, out_ref):
    full = jnp.float32
    cut = top2.shape[0]
    out_ref[:cut, :] = own_ref[:cut, :] + near[:cut, :].astype(full) + top2[...].astype(full)
    low = low2[...].astype(full) + low3[...].astype(full)
    out_ref[cut:, :] = own_ref[cut:, :] + near[cut:, :].astype(full) + low


def call(kernel, args, outs, fast_out=True, raw=False, sems=0):
    ints = [x.dtype == jnp.int32 for x in args]
    space = pltpu.HBM if raw else pltpu.VMEM
    args = [
        x if flag else pltpu.with_memory_space_constraint(x, space) for x, flag in zip(args, ints)
    ]
    there = pl.BlockSpec(memory_space=space)
    return pl.pallas_call(
        kernel,
        in_specs=[SMEM if flag else there for flag in ints],
        out_specs=[VMEM] * len(outs),
        out_shape=[
            pltpu.VMEM(shape, kind) if fast_out else jax.ShapeDtypeStruct(shape, kind)
            for shape, kind in outs
        ],
        scratch_shapes=[pltpu.SemaphoreType.DMA((sems,))] if sems else [],
        compiler_params=pltpu.CompilerParams(vmem_limit_bytes=16 << 20),
    )(*args)


def few_slabs(
    slabs,
    grad_out,
    w_out,
    query_proj,
    key_proj,
    value_proj,
    w_query,
    w_key,
    w_value,
    tile_keys,
):
    rows, cols = grad_out.shape
    size = query_proj.shape[1]
    half, full = jnp.bfloat16, jnp.float32
    cut, feature_cut = rows // 2, 448

    def to_chip(x, step):
        return lax.ppermute(x, "tp", [(t, t ^ (2 * step)) for t in range(8)])

    def to_mate(x):
        return lax.ppermute(x, "tp", [(t, t ^ 1) for t in range(8)])

    def to_slab(x, turn):
        return lax.ppermute(x, "ctx", [(c, c ^ turn) for c in range(slabs)])

    def to_beside(x):
        pairs = [(c * 8 + t, (c ^ (1 + t % 2)) * 8 + t) for c in range(slabs) for t in range(8)]
        return lax.ppermute(x, ("ctx", "tp"), pairs)

    top, low = call(
        split_kernel, [grad_out], [((cut, cols), half), ((rows - cut, cols), half)],
        raw=True, sems=2,
    )
    top2 = to_chip(top, 2)
    near = to_chip(grad_out, 1)
    low2 = to_chip(low, 2)
    low3 = to_chip(low, 3)
    top3 = to_chip(top2, 1)
    pack, near_out = call(
        pack_kernel, [query_proj, key_proj, value_proj, w_out],
        [((rows, 3 * size), half), ((size, 4 * cols), half)], raw=True, sems=7,
    )
    packs = [pack] + [to_slab(pack, turn) for turn in range(1, slabs)]
    mate_out = to_mate(w_out)
    own_w = [w_query, w_key, w_value]
    mate_w = [to_mate(w) for w in own_w]
    prob_row, prob_col, attn_out = call(
        functools.partial(softmax_kernel, slabs, tile_keys.shape[1]),
        [tile_keys, *packs],
        [((rows, slabs * rows), full), ((slabs * rows, rows), full), ((slabs * rows, size), full)],
    )
    (early,) = call(
        functools.partial(attn_grad_kernel, cols, EARLY),
        [top, low, near] + ([top2, low2] if 2 in EARLY else []) + [near_out, mate_out],
        [((rows, 2 * size), full)],
    )
    late = tuple(step for step in range(4) if step not in EARLY)
    (part,) = call(
        functools.partial(attn_grad_kernel, cols, late),
        ([] if 2 in EARLY else [top2, low2]) + [top3, low3, near_out, mate_out, early],
        [((rows, 2 * size), full)],
    )
    both, grad = call(
        merge_kernel, [part, to_mate(part)],
        [((rows, 2 * size), half), ((rows, size), half)],
    )
    beside = to_beside(both)
    across = to_slab(grad, 3)
    swapped = to_mate(beside)
    (d_query,) = call(
        functools.partial(query_grad_kernel, slabs),
        [grad, *packs, prob_row, attn_out],
        [((rows, size), half)],
    )
    (own_grads,) = call(
        functools.partial(key_grad_kernel, slabs),
        [grad, beside, swapped, across, *packs, d_query, prob_col, attn_out],
        [((rows, 3 * size), half)],
    )
    mate_grads = to_mate(own_grads)
    (own_sums,) = call(
        functools.partial(project_own_kernel, cols), [own_grads, *own_w], [((4 * cols, rows), full)]
    )


    def project(step, first, count, kind, *fed):
        (part,) = call(
            functools.partial(project_kernel, cols, step, first),
            [own_sums, mate_grads, *mate_w, *fed],
            [((count, rows), kind)],
        )
        return part

    rest = cols - feature_cut
    fed = to_chip(project(3, 0, feature_cut, half), 1)
    low3 = to_chip(project(3, feature_cut, rest, half), 3)
    low2 = to_chip(project(2, feature_cut, rest, half), 2)
    near = to_chip(project(1, 0, cols, half), 1)
    top2 = to_chip(project(2, 0, feature_cut, half, fed), 2)
    (out,) = call(
        sum_kernel,
        [project(0, 0, cols, full), near, top2, low2, low3],
        [((cols, rows), full)],
        fast_out=False,
    )
    return out


def solution(mesh):
    slabs, shards = mesh.shape["ctx"], mesh.shape["tp"]
    few = slabs == 4 and shards == 8
    return jax.shard_map(
        functools.partial(few_slabs, slabs) if few else many_slabs,
        mesh=mesh,
        in_specs=(
            P("ctx", "tp"),
            P("tp", None),
            P("ctx", "tp"),
            P("ctx", "tp"),
            P("ctx", "tp"),
            P(None, "tp"),
            P(None, "tp"),
            P(None, "tp"),
            P(),
        ),
        out_specs=P("tp", "ctx"),
        check_vma=False,
    )
```

```python
import functools

import jax
import jax.numpy as jnp
from jax import lax
from jax.experimental import pallas as pl
from jax.experimental.pallas import tpu as pltpu
from jax.sharding import PartitionSpec as P


TILE = 128
PIECES = 2
EARLY = (0, 1, 2)
CONTRACT_LAST = (((1,), (1,)), ((), ()))
CONTRACT_FIRST = (((0,), (0,)), ((), ()))
VMEM = pl.BlockSpec(memory_space=pltpu.VMEM)
SMEM = pl.BlockSpec(memory_space=pltpu.SMEM)


def dot_f32(a, b, dims):
    return lax.dot_general(a, b, dims, preferred_element_type=jnp.float32)


def many_slabs(
    grad_out, w_out, query_proj, key_proj, value_proj, w_query, w_key, w_value, tile_keys
):
    row_count = query_proj.shape[0]
    head_size = query_proj.shape[1]
    score_scale = head_size ** (-0.5)
    tiles_here = row_count // TILE
    slab_index = lax.axis_index("ctx")
    d_attn = dot_f32(
        lax.all_gather(grad_out, "tp", axis=1, tiled=True), w_out, CONTRACT_LAST
    ).astype(jnp.bfloat16)
    keys_all, values_all = (
        lax.all_gather(key_proj, "ctx", axis=0, tiled=True),
        lax.all_gather(value_proj, "ctx", axis=0, tiled=True),
    )
    total_tiles = keys_all.shape[0] // TILE
    own_lists = lax.dynamic_slice_in_dim(tile_keys, slab_index * tiles_here, tiles_here, 0)
    all_tiles = jnp.arange(total_tiles, dtype=jnp.int32)
    tile_ok = jnp.any(own_lists[:, :, None] == all_tiles[None, None, :], axis=1)
    token_mask = jnp.repeat(jnp.repeat(tile_ok, TILE, axis=0), TILE, axis=1)
    scores = dot_f32(query_proj, keys_all, CONTRACT_LAST) * score_scale
    scores = jnp.where(token_mask, scores, -jnp.inf)
    row_max = jnp.max(scores, axis=1, keepdims=True)
    exponent = jnp.exp(scores - row_max)
    row_total = jnp.sum(exponent, axis=1, keepdims=True)
    prob_exact = exponent / row_total
    prob_half = prob_exact.astype(jnp.bfloat16)
    attn_out = jnp.dot(prob_half, values_all, preferred_element_type=jnp.float32)
    row_delta = jnp.sum(d_attn.astype(jnp.float32) * attn_out, axis=1, keepdims=True)
    d_prob = dot_f32(d_attn, values_all, CONTRACT_LAST)
    d_score = (prob_exact * (d_prob - row_delta) * score_scale).astype(jnp.bfloat16)
    d_query = jnp.dot(d_score, keys_all, preferred_element_type=jnp.float32).astype(jnp.bfloat16)
    key_part = dot_f32(d_score, query_proj, CONTRACT_FIRST)
    value_part = dot_f32(prob_half, d_attn, CONTRACT_FIRST)
    key_sums = lax.psum_scatter(
        jnp.concatenate([key_part, value_part], axis=1), "ctx", scatter_dimension=0, tiled=True
    )
    d_key = key_sums[:, :head_size].astype(jnp.bfloat16)
    d_value = key_sums[:, head_size:].astype(jnp.bfloat16)
    feature_sum = dot_f32(w_query, d_query, CONTRACT_LAST)
    feature_sum = feature_sum + dot_f32(w_key, d_key, CONTRACT_LAST)
    feature_sum = feature_sum + dot_f32(w_value, d_value, CONTRACT_LAST)
    return lax.psum_scatter(feature_sum, "tp", scatter_dimension=0, tiled=True)


def pack_kernel(query_ref, key_ref, value_ref, w_ref, out_ref, w_out_ref, sems):
    size = query_ref.shape[1]
    copies = [
        pltpu.make_async_copy(
            part, out_ref.at[:, place * size : (place + 1) * size], sems.at[place]
        )
        for place, part in enumerate((query_ref, key_ref, value_ref))
    ]
    cols = w_out_ref.shape[1] // 4
    for step in range(4):
        start = pl.multiple_of((lax.axis_index("tp") ^ (2 * step)) * cols, 128)
        copies.append(
            pltpu.make_async_copy(
                w_ref.at[:, pl.ds(start, cols)],
                w_out_ref.at[:, step * cols : (step + 1) * cols],
                sems.at[3 + step],
            )
        )
    for copy in copies:
        copy.start()
    for copy in copies:
        copy.wait()


def split_kernel(whole_ref, *refs):
    outs, sems = refs[:-1], refs[-1]
    copies, start = [], 0
    for place, out in enumerate(outs):
        step = out.shape[0] // PIECES
        for piece in range(PIECES):
            copies.append(
                pltpu.make_async_copy(
                    whole_ref.at[pl.ds(start + piece * step, step)],
                    out.at[pl.ds(piece * step, step)],
                    sems.at[place * PIECES + piece],
                )
            )
        start += out.shape[0]
    for copy in copies:
        copy.start()
    for copy in copies:
        copy.wait()


def attn_grad_kernel(cols, steps, results, *refs):
    index = lax.axis_index("tp")
    count = sum(1 if step == 1 else 2 for step in steps)
    refs, outs = refs[:-results], refs[-results:]
    parts, own_w, mate_w = list(refs[:count]), refs[count], refs[count + 1]
    total = refs[-1][...] if len(refs) > count + 2 else None
    for step in steps:
        start = pl.multiple_of((index ^ (2 * step)) * cols, 128)
        weight = jnp.concatenate(
            [own_w[:, step * cols : (step + 1) * cols], mate_w[:, pl.ds(start, cols)]], axis=0
        )
        pieces = [parts.pop(0)[...] for _ in range(1 if step == 1 else 2)]
        block = jnp.concatenate(pieces, axis=0)
        term = dot_f32(block, weight, CONTRACT_LAST)
        total = term if total is None else total + term
    for out in outs:
        out[...] = total.astype(out.dtype)


def merge_kernel(own_ref, mate_ref, out_ref, own_out_ref):
    size = own_out_ref.shape[1]
    own = (own_ref[:, :size] + mate_ref[:, size:]).astype(jnp.bfloat16)
    out_ref[:, :size] = own
    out_ref[:, size:] = (own_ref[:, size:] + mate_ref[:, :size]).astype(jnp.bfloat16)
    own_out_ref[...] = own


def softmax_kernel(slabs, keep, lists_ref, *refs):
    packs = refs[:slabs]
    row_ref, col_ref, attn_ref = refs[slabs:]
    rows = packs[0].shape[0]
    size = packs[0].shape[1] // 3
    tiles = rows // TILE
    slab = lax.axis_index("ctx")
    scale = size ** (-0.5)
    keys = jnp.concatenate([pack[:, size : 2 * size] for pack in packs], axis=0)
    values = jnp.concatenate([pack[:, 2 * size :] for pack in packs], axis=0)
    for turn in range(slabs):
        for tile in range(tiles):
            query_tile = (slab ^ turn) * tiles + tile
            span = pl.ds(turn * rows + tile * TILE, TILE)
            scores = dot_f32(packs[turn][pl.ds(tile * TILE, TILE), :size], keys, CONTRACT_LAST)
            scores = scores * scale
            parts = []
            for other in range(slabs * tiles):
                key_tile = (slab ^ (other // tiles)) * tiles + other % tiles
                listed = lists_ref[query_tile, 0] == key_tile
                for place in range(1, keep):
                    listed = listed | (lists_ref[query_tile, place] == key_tile)
                part = scores[:, other * TILE : (other + 1) * TILE]
                parts.append(jnp.where(listed, part, -jnp.inf))
            scores = jnp.concatenate(parts, axis=1)
            exponent = jnp.exp(scores - jnp.max(scores, axis=1, keepdims=True))
            prob = exponent * (1.0 / jnp.sum(exponent, axis=1, keepdims=True))
            attn_ref[span, :] = jnp.dot(
                prob.astype(jnp.bfloat16), values, preferred_element_type=jnp.float32
            )
            col_ref[span, :] = prob[:, :rows]
            if turn == 0:
                row_ref[pl.ds(tile * TILE, TILE), :] = prob


def query_grad_kernel(slabs, grad_ref, *refs):
    packs = refs[:slabs]
    row_ref, attn_ref, out_ref = refs[slabs:]
    rows = packs[0].shape[0]
    size = packs[0].shape[1] // 3
    scale = size ** (-0.5)
    grad = grad_ref[...]
    keys = jnp.concatenate([pack[:, size : 2 * size] for pack in packs], axis=0)
    values = jnp.concatenate([pack[:, 2 * size :] for pack in packs], axis=0)
    delta = jnp.sum(grad.astype(jnp.float32) * attn_ref[:rows, :], axis=1, keepdims=True)
    d_prob = dot_f32(grad, values, CONTRACT_LAST)
    d_score = (row_ref[...] * (d_prob - delta) * scale).astype(jnp.bfloat16)
    out_ref[...] = jnp.dot(d_score, keys, preferred_element_type=jnp.float32).astype(jnp.bfloat16)


def key_grad_kernel(slabs, own, beside, swapped, across, *refs):
    packs = refs[:slabs]
    query_ref, col_ref, attn_ref, out_ref = refs[slabs:]
    size = packs[0].shape[1] // 3
    scale = size ** (-0.5)
    even = (lax.axis_index("tp") & 1) == 0
    near, far = beside[:, :size], swapped[:, size:]
    first, second = jnp.where(even, near, far), jnp.where(even, far, near)
    queries = jnp.concatenate([pack[:, :size] for pack in packs], axis=0)
    grad = jnp.concatenate([own[...], first, second, across[...]], axis=0)
    prob = col_ref[...]
    delta = jnp.sum(grad.astype(jnp.float32) * attn_ref[...], axis=1, keepdims=True)
    d_prob = dot_f32(grad, packs[0][:, 2 * size :], CONTRACT_LAST)
    d_score = (prob * (d_prob - delta) * scale).astype(jnp.bfloat16)
    out_ref[:, :size] = query_ref[...]
    out_ref[:, size : 2 * size] = dot_f32(d_score, queries, CONTRACT_FIRST).astype(jnp.bfloat16)
    out_ref[:, 2 * size :] = dot_f32(prob.astype(jnp.bfloat16), grad, CONTRACT_FIRST).astype(
        jnp.bfloat16
    )


def project_own_kernel(block, own_ref, *refs):
    weights, out_ref = refs[:3], refs[3]
    size = own_ref.shape[1] // 3
    for step in range(out_ref.shape[0] // block):
        start = pl.multiple_of((lax.axis_index("tp") ^ (2 * step)) * block, 16)
        total = None
        for place, weight in enumerate(weights):
            part = own_ref[:, place * size : (place + 1) * size]
            term = dot_f32(weight[pl.ds(start, block), :], part, CONTRACT_LAST)
            total = term if total is None else total + term
        out_ref[step * block : (step + 1) * block, :] = total


def project_kernel(block, step, first, own_ref, mate_ref, *refs):
    weights, out_ref = refs[:3], refs[-1]
    rows = out_ref.shape[0]
    start = pl.multiple_of((lax.axis_index("tp") ^ (2 * step)) * block + first, 16)
    size = mate_ref.shape[1] // 3
    total = own_ref[step * block + first : step * block + first + rows, :]
    for place, weight in enumerate(weights):
        part = mate_ref[:, place * size : (place + 1) * size]
        total = total + dot_f32(weight[pl.ds(start, rows), :], part, CONTRACT_LAST)
    for fed in refs[3:-1]:
        total = total + fed[...].astype(jnp.float32)
    out_ref[...] = total.astype(out_ref.dtype)


def sum_kernel(own_ref, near, top2, low2, low3, out_ref):
    full = jnp.float32
    cut = top2.shape[0]
    out_ref[:cut, :] = own_ref[:cut, :] + near[:cut, :].astype(full) + top2[...].astype(full)
    low = low2[...].astype(full) + low3[...].astype(full)
    out_ref[cut:, :] = own_ref[cut:, :] + near[cut:, :].astype(full) + low


def call(kernel, args, outs, fast_out=True, raw=False, sems=0):
    ints = [x.dtype == jnp.int32 for x in args]
    space = pltpu.HBM if raw else pltpu.VMEM
    args = [
        x if flag else pltpu.with_memory_space_constraint(x, space) for x, flag in zip(args, ints)
    ]
    there = pl.BlockSpec(memory_space=space)
    return pl.pallas_call(
        kernel,
        in_specs=[SMEM if flag else there for flag in ints],
        out_specs=[VMEM] * len(outs),
        out_shape=[
            pltpu.VMEM(shape, kind) if fast_out else jax.ShapeDtypeStruct(shape, kind)
            for shape, kind in outs
        ],
        scratch_shapes=[pltpu.SemaphoreType.DMA((sems,))] if sems else [],
        compiler_params=pltpu.CompilerParams(vmem_limit_bytes=16 << 20),
    )(*args)


def few_slabs(
    slabs,
    grad_out,
    w_out,
    query_proj,
    key_proj,
    value_proj,
    w_query,
    w_key,
    w_value,
    tile_keys,
):
    rows, cols = grad_out.shape
    size = query_proj.shape[1]
    half, full = jnp.bfloat16, jnp.float32
    cut, feature_cut = rows // 2, 448

    def to_chip(x, step):
        return lax.ppermute(x, "tp", [(t, t ^ (2 * step)) for t in range(8)])

    def to_mate(x):
        return lax.ppermute(x, "tp", [(t, t ^ 1) for t in range(8)])

    def to_slab(x, turn):
        return lax.ppermute(x, "ctx", [(c, c ^ turn) for c in range(slabs)])

    def to_beside(x):
        pairs = [(c * 8 + t, (c ^ (1 + t % 2)) * 8 + t) for c in range(slabs) for t in range(8)]
        return lax.ppermute(x, ("ctx", "tp"), pairs)

    top, low = call(
        split_kernel, [grad_out], [((cut, cols), half), ((rows - cut, cols), half)],
        raw=True, sems=2 * PIECES,
    )
    top2 = to_chip(top, 2)
    near = to_chip(grad_out, 1)
    low2 = to_chip(low, 2)
    low3 = to_chip(low, 3)
    top3 = to_chip(top2, 1)
    pack, near_out = call(
        pack_kernel, [query_proj, key_proj, value_proj, w_out],
        [((rows, 3 * size), half), ((size, 4 * cols), half)], raw=True, sems=7,
    )
    packs = [pack] + [to_slab(pack, turn) for turn in range(1, slabs)]
    mate_out = to_mate(w_out)
    own_w = [w_query, w_key, w_value]
    mate_w = [to_mate(w) for w in own_w]
    prob_row, prob_col, attn_out = call(
        functools.partial(softmax_kernel, slabs, tile_keys.shape[1]),
        [tile_keys, *packs],
        [((rows, slabs * rows), full), ((slabs * rows, rows), full), ((slabs * rows, size), full)],
    )
    (early,) = call(
        functools.partial(attn_grad_kernel, cols, EARLY, 1),
        [top, low, near] + ([top2, low2] if 2 in EARLY else []) + [near_out, mate_out],
        [((rows, 2 * size), full)],
    )
    late = tuple(step for step in range(4) if step not in EARLY)
    part, narrow = call(
        functools.partial(attn_grad_kernel, cols, late, 2),
        ([] if 2 in EARLY else [top2, low2]) + [top3, low3, near_out, mate_out, early],
        [((rows, 2 * size), full), ((rows, 2 * size), half)],
    )
    both, grad = call(
        merge_kernel, [part, to_mate(narrow)],
        [((rows, 2 * size), half), ((rows, size), half)],
    )
    beside = to_beside(both)
    across = to_slab(grad, 3)
    swapped = to_mate(beside)
    (d_query,) = call(
        functools.partial(query_grad_kernel, slabs),
        [grad, *packs, prob_row, attn_out],
        [((rows, size), half)],
    )
    (own_grads,) = call(
        functools.partial(key_grad_kernel, slabs),
        [grad, beside, swapped, across, *packs, d_query, prob_col, attn_out],
        [((rows, 3 * size), half)],
    )
    mate_grads = to_mate(own_grads)
    (own_sums,) = call(
        functools.partial(project_own_kernel, cols), [own_grads, *own_w], [((4 * cols, rows), full)]
    )


    def project(step, first, count, kind, *fed):
        (part,) = call(
            functools.partial(project_kernel, cols, step, first),
            [own_sums, mate_grads, *mate_w, *fed],
            [((count, rows), kind)],
        )
        return part

    rest = cols - feature_cut
    fed = to_chip(project(3, 0, feature_cut, half), 1)
    low3 = to_chip(project(3, feature_cut, rest, half), 3)
    low2 = to_chip(project(2, feature_cut, rest, half), 2)
    near = to_chip(project(1, 0, cols, half), 1)
    top2 = to_chip(project(2, 0, feature_cut, half, fed), 2)
    (out,) = call(
        sum_kernel,
        [project(0, 0, cols, full), near, top2, low2, low3],
        [((cols, rows), full)],
        fast_out=False,
    )
    return out


def solution(mesh):
    slabs, shards = mesh.shape["ctx"], mesh.shape["tp"]
    few = slabs == 4 and shards == 8
    return jax.shard_map(
        functools.partial(few_slabs, slabs) if few else many_slabs,
        mesh=mesh,
        in_specs=(
            P("ctx", "tp"),
            P("tp", None),
            P("ctx", "tp"),
            P("ctx", "tp"),
            P("ctx", "tp"),
            P(None, "tp"),
            P(None, "tp"),
            P(None, "tp"),
            P(),
        ),
        out_specs=P("tp", "ctx"),
        check_vma=False,
    )
```

```python
import functools

import jax
import jax.numpy as jnp
from jax import lax
from jax.experimental import pallas as pl
from jax.experimental.pallas import tpu as pltpu
from jax.sharding import PartitionSpec as P


TILE = 128
PIECES = 2
EARLY = (0, 1, 2)
CONTRACT_LAST = (((1,), (1,)), ((), ()))
CONTRACT_FIRST = (((0,), (0,)), ((), ()))
VMEM = pl.BlockSpec(memory_space=pltpu.VMEM)
SMEM = pl.BlockSpec(memory_space=pltpu.SMEM)


def dot_f32(a, b, dims):
    return lax.dot_general(a, b, dims, preferred_element_type=jnp.float32)


def many_slabs(
    grad_out, w_out, query_proj, key_proj, value_proj, w_query, w_key, w_value, tile_keys
):
    row_count = query_proj.shape[0]
    head_size = query_proj.shape[1]
    score_scale = head_size ** (-0.5)
    tiles_here = row_count // TILE
    slab_index = lax.axis_index("ctx")
    d_attn = dot_f32(
        lax.all_gather(grad_out, "tp", axis=1, tiled=True), w_out, CONTRACT_LAST
    ).astype(jnp.bfloat16)
    keys_all, values_all = (
        lax.all_gather(key_proj, "ctx", axis=0, tiled=True),
        lax.all_gather(value_proj, "ctx", axis=0, tiled=True),
    )
    total_tiles = keys_all.shape[0] // TILE
    own_lists = lax.dynamic_slice_in_dim(tile_keys, slab_index * tiles_here, tiles_here, 0)
    all_tiles = jnp.arange(total_tiles, dtype=jnp.int32)
    tile_ok = jnp.any(own_lists[:, :, None] == all_tiles[None, None, :], axis=1)
    token_mask = jnp.repeat(jnp.repeat(tile_ok, TILE, axis=0), TILE, axis=1)
    scores = dot_f32(query_proj, keys_all, CONTRACT_LAST) * score_scale
    scores = jnp.where(token_mask, scores, -jnp.inf)
    row_max = jnp.max(scores, axis=1, keepdims=True)
    exponent = jnp.exp(scores - row_max)
    row_total = jnp.sum(exponent, axis=1, keepdims=True)
    prob_exact = exponent / row_total
    prob_half = prob_exact.astype(jnp.bfloat16)
    attn_out = jnp.dot(prob_half, values_all, preferred_element_type=jnp.float32)
    row_delta = jnp.sum(d_attn.astype(jnp.float32) * attn_out, axis=1, keepdims=True)
    d_prob = dot_f32(d_attn, values_all, CONTRACT_LAST)
    d_score = (prob_exact * (d_prob - row_delta) * score_scale).astype(jnp.bfloat16)
    d_query = jnp.dot(d_score, keys_all, preferred_element_type=jnp.float32).astype(jnp.bfloat16)
    key_part = dot_f32(d_score, query_proj, CONTRACT_FIRST)
    value_part = dot_f32(prob_half, d_attn, CONTRACT_FIRST)
    key_sums = lax.psum_scatter(
        jnp.concatenate([key_part, value_part], axis=1), "ctx", scatter_dimension=0, tiled=True
    )
    d_key = key_sums[:, :head_size].astype(jnp.bfloat16)
    d_value = key_sums[:, head_size:].astype(jnp.bfloat16)
    feature_sum = dot_f32(w_query, d_query, CONTRACT_LAST)
    feature_sum = feature_sum + dot_f32(w_key, d_key, CONTRACT_LAST)
    feature_sum = feature_sum + dot_f32(w_value, d_value, CONTRACT_LAST)
    return lax.psum_scatter(feature_sum, "tp", scatter_dimension=0, tiled=True)


def pack_kernel(query_ref, key_ref, value_ref, w_ref, out_ref, w_out_ref, sems):
    size = query_ref.shape[1]
    copies = [
        pltpu.make_async_copy(
            part, out_ref.at[:, place * size : (place + 1) * size], sems.at[place]
        )
        for place, part in enumerate((query_ref, key_ref, value_ref))
    ]
    cols = w_out_ref.shape[1] // 4
    for step in range(4):
        start = pl.multiple_of((lax.axis_index("tp") ^ (2 * step)) * cols, 128)
        copies.append(
            pltpu.make_async_copy(
                w_ref.at[:, pl.ds(start, cols)],
                w_out_ref.at[:, step * cols : (step + 1) * cols],
                sems.at[3 + step],
            )
        )
    for copy in copies:
        copy.start()
    for copy in copies:
        copy.wait()


def split_kernel(whole_ref, *refs):
    outs, sems = refs[:-1], refs[-1]
    copies, start = [], 0
    for place, out in enumerate(outs):
        step = out.shape[0] // PIECES
        for piece in range(PIECES):
            copies.append(
                pltpu.make_async_copy(
                    whole_ref.at[pl.ds(start + piece * step, step)],
                    out.at[pl.ds(piece * step, step)],
                    sems.at[place * PIECES + piece],
                )
            )
        start += out.shape[0]
    for copy in copies:
        copy.start()
    for copy in copies:
        copy.wait()


def attn_grad_kernel(cols, steps, *refs):
    index = lax.axis_index("tp")
    count = sum(1 if step == 1 else 2 for step in steps)
    parts, own_w, mate_w, out_ref = list(refs[:count]), refs[count], refs[count + 1], refs[-1]
    total = refs[-2][...] if len(refs) > count + 3 else None
    for step in steps:
        start = pl.multiple_of((index ^ (2 * step)) * cols, 128)
        weight = jnp.concatenate(
            [own_w[:, step * cols : (step + 1) * cols], mate_w[:, pl.ds(start, cols)]], axis=0
        )
        pieces = [parts.pop(0)[...] for _ in range(1 if step == 1 else 2)]
        block = jnp.concatenate(pieces, axis=0)
        term = dot_f32(block, weight, CONTRACT_LAST)
        total = term if total is None else total + term
    out_ref[...] = total


def merge_kernel(own_ref, mate_ref, out_ref, own_out_ref):
    size = own_out_ref.shape[1]
    own = (own_ref[:, :size] + mate_ref[:, size:]).astype(jnp.bfloat16)
    out_ref[:, :size] = own
    out_ref[:, size:] = (own_ref[:, size:] + mate_ref[:, :size]).astype(jnp.bfloat16)
    own_out_ref[...] = own


def softmax_kernel(slabs, keep, lists_ref, *refs):
    packs = refs[:slabs]
    row_ref, col_ref, attn_ref = refs[slabs:]
    rows = packs[0].shape[0]
    size = packs[0].shape[1] // 3
    tiles = rows // TILE
    slab = lax.axis_index("ctx")
    scale = size ** (-0.5)
    keys = jnp.concatenate([pack[:, size : 2 * size] for pack in packs], axis=0)
    values = jnp.concatenate([pack[:, 2 * size :] for pack in packs], axis=0)
    for turn in range(slabs):
        for tile in range(tiles):
            query_tile = (slab ^ turn) * tiles + tile
            span = pl.ds(turn * rows + tile * TILE, TILE)
            scores = dot_f32(packs[turn][pl.ds(tile * TILE, TILE), :size], keys, CONTRACT_LAST)
            scores = scores * scale
            parts = []
            for other in range(slabs * tiles):
                key_tile = (slab ^ (other // tiles)) * tiles + other % tiles
                listed = lists_ref[query_tile, 0] == key_tile
                for place in range(1, keep):
                    listed = listed | (lists_ref[query_tile, place] == key_tile)
                part = scores[:, other * TILE : (other + 1) * TILE]
                parts.append(jnp.where(listed, part, -jnp.inf))
            scores = jnp.concatenate(parts, axis=1)
            exponent = jnp.exp(scores - jnp.max(scores, axis=1, keepdims=True))
            prob = exponent * (1.0 / jnp.sum(exponent, axis=1, keepdims=True))
            attn_ref[span, :] = jnp.dot(
                prob.astype(jnp.bfloat16), values, preferred_element_type=jnp.float32
            )
            col_ref[span, :] = prob[:, :rows]
            if turn == 0:
                row_ref[pl.ds(tile * TILE, TILE), :] = prob


def query_grad_kernel(slabs, grad_ref, *refs):
    packs = refs[:slabs]
    row_ref, attn_ref, out_ref = refs[slabs:]
    rows = packs[0].shape[0]
    size = packs[0].shape[1] // 3
    scale = size ** (-0.5)
    grad = grad_ref[...]
    keys = jnp.concatenate([pack[:, size : 2 * size] for pack in packs], axis=0)
    values = jnp.concatenate([pack[:, 2 * size :] for pack in packs], axis=0)
    delta = jnp.sum(grad.astype(jnp.float32) * attn_ref[:rows, :], axis=1, keepdims=True)
    d_prob = dot_f32(grad, values, CONTRACT_LAST)
    d_score = (row_ref[...] * (d_prob - delta) * scale).astype(jnp.bfloat16)
    out_ref[...] = jnp.dot(d_score, keys, preferred_element_type=jnp.float32).astype(jnp.bfloat16)


def key_grad_kernel(slabs, own, beside, swapped, across, *refs):
    packs = refs[:slabs]
    query_ref, col_ref, attn_ref, out_ref = refs[slabs:]
    size = packs[0].shape[1] // 3
    scale = size ** (-0.5)
    even = (lax.axis_index("tp") & 1) == 0
    near, far = beside[:, :size], swapped[:, size:]
    first, second = jnp.where(even, near, far), jnp.where(even, far, near)
    queries = jnp.concatenate([pack[:, :size] for pack in packs], axis=0)
    grad = jnp.concatenate([own[...], first, second, across[...]], axis=0)
    prob = col_ref[...]
    delta = jnp.sum(grad.astype(jnp.float32) * attn_ref[...], axis=1, keepdims=True)
    d_prob = dot_f32(grad, packs[0][:, 2 * size :], CONTRACT_LAST)
    d_score = (prob * (d_prob - delta) * scale).astype(jnp.bfloat16)
    out_ref[:, :size] = query_ref[...]
    out_ref[:, size : 2 * size] = dot_f32(d_score, queries, CONTRACT_FIRST).astype(jnp.bfloat16)
    out_ref[:, 2 * size :] = dot_f32(prob.astype(jnp.bfloat16), grad, CONTRACT_FIRST).astype(
        jnp.bfloat16
    )


def project_own_kernel(block, own_ref, *refs):
    weights, out_ref = refs[:3], refs[3]
    size = own_ref.shape[1] // 3
    for step in range(out_ref.shape[0] // block):
        start = pl.multiple_of((lax.axis_index("tp") ^ (2 * step)) * block, 16)
        total = None
        for place, weight in enumerate(weights):
            part = own_ref[:, place * size : (place + 1) * size]
            term = dot_f32(weight[pl.ds(start, block), :], part, CONTRACT_LAST)
            total = term if total is None else total + term
        out_ref[step * block : (step + 1) * block, :] = total


def project_kernel(block, step, first, own_ref, mate_ref, *refs):
    weights, out_ref = refs[:3], refs[-1]
    rows = out_ref.shape[0]
    start = pl.multiple_of((lax.axis_index("tp") ^ (2 * step)) * block + first, 16)
    size = mate_ref.shape[1] // 3
    total = own_ref[step * block + first : step * block + first + rows, :]
    for place, weight in enumerate(weights):
        part = mate_ref[:, place * size : (place + 1) * size]
        total = total + dot_f32(weight[pl.ds(start, rows), :], part, CONTRACT_LAST)
    for fed in refs[3:-1]:
        total = total + fed[...].astype(jnp.float32)
    out_ref[...] = total.astype(out_ref.dtype)


def sum_kernel(own_ref, near, top2, low2, low3, out_ref):
    full = jnp.float32
    cut = top2.shape[0]
    out_ref[:cut, :] = own_ref[:cut, :] + near[:cut, :].astype(full) + top2[...].astype(full)
    low = low2[...].astype(full) + low3[...].astype(full)
    out_ref[cut:, :] = own_ref[cut:, :] + near[cut:, :].astype(full) + low


def call(kernel, args, outs, fast_out=True, raw=False, sems=0):
    ints = [x.dtype == jnp.int32 for x in args]
    space = pltpu.HBM if raw else pltpu.VMEM
    args = [
        x if flag else pltpu.with_memory_space_constraint(x, space) for x, flag in zip(args, ints)
    ]
    there = pl.BlockSpec(memory_space=space)
    return pl.pallas_call(
        kernel,
        in_specs=[SMEM if flag else there for flag in ints],
        out_specs=[VMEM] * len(outs),
        out_shape=[
            pltpu.VMEM(shape, kind) if fast_out else jax.ShapeDtypeStruct(shape, kind)
            for shape, kind in outs
        ],
        scratch_shapes=[pltpu.SemaphoreType.DMA((sems,))] if sems else [],
        compiler_params=pltpu.CompilerParams(vmem_limit_bytes=16 << 20),
    )(*args)


def few_slabs(
    slabs,
    grad_out,
    w_out,
    query_proj,
    key_proj,
    value_proj,
    w_query,
    w_key,
    w_value,
    tile_keys,
):
    rows, cols = grad_out.shape
    size = query_proj.shape[1]
    half, full = jnp.bfloat16, jnp.float32
    cut, feature_cut = rows // 2, 448

    def to_chip(x, step):
        return lax.ppermute(x, "tp", [(t, t ^ (2 * step)) for t in range(8)])

    def to_mate(x):
        return lax.ppermute(x, "tp", [(t, t ^ 1) for t in range(8)])

    def to_slab(x, turn):
        return lax.ppermute(x, "ctx", [(c, c ^ turn) for c in range(slabs)])

    def to_beside(x):
        pairs = [(c * 8 + t, (c ^ (1 + t % 2)) * 8 + t) for c in range(slabs) for t in range(8)]
        return lax.ppermute(x, ("ctx", "tp"), pairs)

    top, low = call(
        split_kernel, [grad_out], [((cut, cols), half), ((rows - cut, cols), half)],
        raw=True, sems=2 * PIECES,
    )
    top2 = to_chip(top, 2)
    near = to_chip(grad_out, 1)
    low2 = to_chip(low, 2)
    low3 = to_chip(low, 3)
    top3 = to_chip(top2, 1)
    pack, near_out = call(
        pack_kernel, [query_proj, key_proj, value_proj, w_out],
        [((rows, 3 * size), half), ((size, 4 * cols), half)], raw=True, sems=7,
    )
    packs = [pack] + [to_slab(pack, turn) for turn in range(1, slabs)]
    mate_out = to_mate(w_out)
    own_w = [w_query, w_key, w_value]
    mate_w = [to_mate(w) for w in own_w]
    prob_row, prob_col, attn_out = call(
        functools.partial(softmax_kernel, slabs, tile_keys.shape[1]),
        [tile_keys, *packs],
        [((rows, slabs * rows), full), ((slabs * rows, rows), full), ((slabs * rows, size), full)],
    )
    (early,) = call(
        functools.partial(attn_grad_kernel, cols, EARLY),
        [top, low, near] + ([top2, low2] if 2 in EARLY else []) + [near_out, mate_out],
        [((rows, 2 * size), full)],
    )
    late = tuple(step for step in range(4) if step not in EARLY)
    (part,) = call(
        functools.partial(attn_grad_kernel, cols, late),
        ([] if 2 in EARLY else [top2, low2]) + [top3, low3, near_out, mate_out, early],
        [((rows, 2 * size), full)],
    )
    both, grad = call(
        merge_kernel, [part, to_mate(part)],
        [((rows, 2 * size), half), ((rows, size), half)],
    )
    beside = to_beside(both)
    across = to_slab(grad, 3)
    swapped = to_mate(beside)
    (d_query,) = call(
        functools.partial(query_grad_kernel, slabs),
        [grad, *packs, prob_row, attn_out],
        [((rows, size), half)],
    )
    (own_grads,) = call(
        functools.partial(key_grad_kernel, slabs),
        [grad, beside, swapped, across, *packs, d_query, prob_col, attn_out],
        [((rows, 3 * size), half)],
    )
    mate_grads = to_mate(own_grads)
    (own_sums,) = call(
        functools.partial(project_own_kernel, cols), [own_grads, *own_w], [((4 * cols, rows), full)]
    )


    def project(step, first, count, kind, *fed):
        (part,) = call(
            functools.partial(project_kernel, cols, step, first),
            [own_sums, mate_grads, *mate_w, *fed],
            [((count, rows), kind)],
        )
        return part

    rest = cols - feature_cut
    fed = to_chip(project(3, 0, feature_cut, half), 1)
    low3 = to_chip(project(3, feature_cut, rest, half), 3)
    low2 = to_chip(project(2, feature_cut, rest, half), 2)
    near = to_chip(project(1, 0, cols, half), 1)
    top2 = to_chip(project(2, 0, feature_cut, half, fed), 2)
    (out,) = call(
        sum_kernel,
        [project(0, 0, cols, full), near, top2, low2, low3],
        [((cols, rows), full)],
        fast_out=False,
    )
    return out


def solution(mesh):
    slabs, shards = mesh.shape["ctx"], mesh.shape["tp"]
    few = slabs == 4 and shards == 8
    return jax.shard_map(
        functools.partial(few_slabs, slabs) if few else many_slabs,
        mesh=mesh,
        in_specs=(
            P("ctx", "tp"),
            P("tp", None),
            P("ctx", "tp"),
            P("ctx", "tp"),
            P("ctx", "tp"),
            P(None, "tp"),
            P(None, "tp"),
            P(None, "tp"),
            P(),
        ),
        out_specs=P("tp", "ctx"),
        check_vma=False,
    )
```

```python
import functools

import jax
import jax.numpy as jnp
from jax import lax
from jax.experimental import pallas as pl
from jax.experimental.pallas import tpu as pltpu
from jax.sharding import PartitionSpec as P


TILE = 128
EARLY = (0, 1, 2)
CONTRACT_LAST = (((1,), (1,)), ((), ()))
CONTRACT_FIRST = (((0,), (0,)), ((), ()))
VMEM = pl.BlockSpec(memory_space=pltpu.VMEM)
SMEM = pl.BlockSpec(memory_space=pltpu.SMEM)


def dot_f32(a, b, dims):
    return lax.dot_general(a, b, dims, preferred_element_type=jnp.float32)


def many_slabs(
    grad_out, w_out, query_proj, key_proj, value_proj, w_query, w_key, w_value, tile_keys
):
    row_count = query_proj.shape[0]
    head_size = query_proj.shape[1]
    score_scale = head_size ** (-0.5)
    tiles_here = row_count // TILE
    slab_index = lax.axis_index("ctx")
    d_attn = dot_f32(
        lax.all_gather(grad_out, "tp", axis=1, tiled=True), w_out, CONTRACT_LAST
    ).astype(jnp.bfloat16)
    keys_all, values_all = (
        lax.all_gather(key_proj, "ctx", axis=0, tiled=True),
        lax.all_gather(value_proj, "ctx", axis=0, tiled=True),
    )
    total_tiles = keys_all.shape[0] // TILE
    own_lists = lax.dynamic_slice_in_dim(tile_keys, slab_index * tiles_here, tiles_here, 0)
    all_tiles = jnp.arange(total_tiles, dtype=jnp.int32)
    tile_ok = jnp.any(own_lists[:, :, None] == all_tiles[None, None, :], axis=1)
    token_mask = jnp.repeat(jnp.repeat(tile_ok, TILE, axis=0), TILE, axis=1)
    scores = dot_f32(query_proj, keys_all, CONTRACT_LAST) * score_scale
    scores = jnp.where(token_mask, scores, -jnp.inf)
    row_max = jnp.max(scores, axis=1, keepdims=True)
    exponent = jnp.exp(scores - row_max)
    row_total = jnp.sum(exponent, axis=1, keepdims=True)
    prob_exact = exponent / row_total
    prob_half = prob_exact.astype(jnp.bfloat16)
    attn_out = jnp.dot(prob_half, values_all, preferred_element_type=jnp.float32)
    row_delta = jnp.sum(d_attn.astype(jnp.float32) * attn_out, axis=1, keepdims=True)
    d_prob = dot_f32(d_attn, values_all, CONTRACT_LAST)
    d_score = (prob_exact * (d_prob - row_delta) * score_scale).astype(jnp.bfloat16)
    d_query = jnp.dot(d_score, keys_all, preferred_element_type=jnp.float32).astype(jnp.bfloat16)
    key_part = dot_f32(d_score, query_proj, CONTRACT_FIRST)
    value_part = dot_f32(prob_half, d_attn, CONTRACT_FIRST)
    key_sums = lax.psum_scatter(
        jnp.concatenate([key_part, value_part], axis=1), "ctx", scatter_dimension=0, tiled=True
    )
    d_key = key_sums[:, :head_size].astype(jnp.bfloat16)
    d_value = key_sums[:, head_size:].astype(jnp.bfloat16)
    feature_sum = dot_f32(w_query, d_query, CONTRACT_LAST)
    feature_sum = feature_sum + dot_f32(w_key, d_key, CONTRACT_LAST)
    feature_sum = feature_sum + dot_f32(w_value, d_value, CONTRACT_LAST)
    return lax.psum_scatter(feature_sum, "tp", scatter_dimension=0, tiled=True)


def pack_kernel(query_ref, key_ref, value_ref, w_ref, out_ref, w_out_ref, sems):
    size = query_ref.shape[1]
    copies = [
        pltpu.make_async_copy(
            part, out_ref.at[:, place * size : (place + 1) * size], sems.at[place]
        )
        for place, part in enumerate((query_ref, key_ref, value_ref))
    ]
    cols = w_out_ref.shape[1] // 4
    for step in range(4):
        start = pl.multiple_of((lax.axis_index("tp") ^ (2 * step)) * cols, 128)
        copies.append(
            pltpu.make_async_copy(
                w_ref.at[:, pl.ds(start, cols)],
                w_out_ref.at[:, step * cols : (step + 1) * cols],
                sems.at[3 + step],
            )
        )
    for copy in copies:
        copy.start()
    for copy in copies:
        copy.wait()


def split_kernel(whole_ref, *refs):
    outs, sems = refs[:-1], refs[-1]
    copies, start = [], 0
    for place, out in enumerate(outs):
        span = pl.ds(start, out.shape[0])
        copies.append(pltpu.make_async_copy(whole_ref.at[span], out, sems.at[place]))
        start += out.shape[0]
    for copy in copies:
        copy.start()
    for copy in copies:
        copy.wait()


def attn_grad_kernel(cols, steps, *refs):
    index = lax.axis_index("tp")
    count = sum(1 if step == 1 else 2 for step in steps)
    parts, own_w, mate_w, out_ref = list(refs[:count]), refs[count], refs[count + 1], refs[-1]
    total = refs[-2][...] if len(refs) > count + 3 else None
    for step in steps:
        start = pl.multiple_of((index ^ (2 * step)) * cols, 128)
        weight = jnp.concatenate(
            [own_w[:, step * cols : (step + 1) * cols], mate_w[:, pl.ds(start, cols)]], axis=0
        )
        pieces = [parts.pop(0)[...] for _ in range(1 if step == 1 else 2)]
        block = jnp.concatenate(pieces, axis=0)
        term = dot_f32(block, weight, CONTRACT_LAST)
        total = term if total is None else total + term
    out_ref[...] = total


def merge_kernel(own_ref, mate_ref, out_ref, own_out_ref):
    size = own_out_ref.shape[1]
    own = (own_ref[:, :size] + mate_ref[:, size:]).astype(jnp.bfloat16)
    out_ref[:, :size] = own
    out_ref[:, size:] = (own_ref[:, size:] + mate_ref[:, :size]).astype(jnp.bfloat16)
    own_out_ref[...] = own


def softmax_kernel(slabs, keep, lists_ref, *refs):
    packs = refs[:slabs]
    row_ref, col_ref, attn_ref = refs[slabs:]
    rows = packs[0].shape[0]
    size = packs[0].shape[1] // 3
    tiles = rows // TILE
    slab = lax.axis_index("ctx")
    scale = size ** (-0.5)
    keys = jnp.concatenate([pack[:, size : 2 * size] for pack in packs], axis=0)
    values = jnp.concatenate([pack[:, 2 * size :] for pack in packs], axis=0)
    for turn in range(slabs):
        for tile in range(tiles):
            query_tile = (slab ^ turn) * tiles + tile
            span = pl.ds(turn * rows + tile * TILE, TILE)
            scores = dot_f32(packs[turn][pl.ds(tile * TILE, TILE), :size], keys, CONTRACT_LAST)
            scores = scores * scale
            parts = []
            for other in range(slabs * tiles):
                key_tile = (slab ^ (other // tiles)) * tiles + other % tiles
                listed = lists_ref[query_tile, 0] == key_tile
                for place in range(1, keep):
                    listed = listed | (lists_ref[query_tile, place] == key_tile)
                part = scores[:, other * TILE : (other + 1) * TILE]
                parts.append(jnp.where(listed, part, -jnp.inf))
            scores = jnp.concatenate(parts, axis=1)
            exponent = jnp.exp(scores - jnp.max(scores, axis=1, keepdims=True))
            prob = exponent * (1.0 / jnp.sum(exponent, axis=1, keepdims=True))
            attn_ref[span, :] = jnp.dot(
                prob.astype(jnp.bfloat16), values, preferred_element_type=jnp.float32
            )
            col_ref[span, :] = prob[:, :rows]
            if turn == 0:
                row_ref[pl.ds(tile * TILE, TILE), :] = prob


def query_grad_kernel(slabs, grad_ref, *refs):
    packs = refs[:slabs]
    row_ref, attn_ref, out_ref = refs[slabs:]
    rows = packs[0].shape[0]
    size = packs[0].shape[1] // 3
    scale = size ** (-0.5)
    grad = grad_ref[...]
    keys = jnp.concatenate([pack[:, size : 2 * size] for pack in packs], axis=0)
    values = jnp.concatenate([pack[:, 2 * size :] for pack in packs], axis=0)
    delta = jnp.sum(grad.astype(jnp.float32) * attn_ref[:rows, :], axis=1, keepdims=True)
    d_prob = dot_f32(grad, values, CONTRACT_LAST)
    d_score = (row_ref[...] * (d_prob - delta) * scale).astype(jnp.bfloat16)
    out_ref[...] = jnp.dot(d_score, keys, preferred_element_type=jnp.float32).astype(jnp.bfloat16)


def key_grad_kernel(slabs, own, beside, swapped, across, *refs):
    packs = refs[:slabs]
    query_ref, col_ref, attn_ref, out_ref = refs[slabs:]
    size = packs[0].shape[1] // 3
    scale = size ** (-0.5)
    even = (lax.axis_index("tp") & 1) == 0
    near, far = beside[:, :size], swapped[:, size:]
    first, second = jnp.where(even, near, far), jnp.where(even, far, near)
    queries = jnp.concatenate([pack[:, :size] for pack in packs], axis=0)
    grad = jnp.concatenate([own[...], first, second, across[...]], axis=0)
    prob = col_ref[...]
    delta = jnp.sum(grad.astype(jnp.float32) * attn_ref[...], axis=1, keepdims=True)
    d_prob = dot_f32(grad, packs[0][:, 2 * size :], CONTRACT_LAST)
    d_score = (prob * (d_prob - delta) * scale).astype(jnp.bfloat16)
    out_ref[:, :size] = query_ref[...]
    out_ref[:, size : 2 * size] = dot_f32(d_score, queries, CONTRACT_FIRST).astype(jnp.bfloat16)
    out_ref[:, 2 * size :] = dot_f32(prob.astype(jnp.bfloat16), grad, CONTRACT_FIRST).astype(
        jnp.bfloat16
    )


def project_own_kernel(block, own_ref, *refs):
    weights, out_ref = refs[:3], refs[3]
    size = own_ref.shape[1] // 3
    for step in range(out_ref.shape[0] // block):
        start = pl.multiple_of((lax.axis_index("tp") ^ (2 * step)) * block, 16)
        total = None
        for place, weight in enumerate(weights):
            part = own_ref[:, place * size : (place + 1) * size]
            term = dot_f32(weight[pl.ds(start, block), :], part, CONTRACT_LAST)
            total = term if total is None else total + term
        out_ref[step * block : (step + 1) * block, :] = total


def project_kernel(block, step, first, own_ref, mate_ref, *refs):
    weights, out_ref = refs[:3], refs[-1]
    rows = out_ref.shape[0]
    start = pl.multiple_of((lax.axis_index("tp") ^ (2 * step)) * block + first, 16)
    size = mate_ref.shape[1] // 3
    total = own_ref[step * block + first : step * block + first + rows, :]
    for place, weight in enumerate(weights):
        part = mate_ref[:, place * size : (place + 1) * size]
        total = total + dot_f32(weight[pl.ds(start, rows), :], part, CONTRACT_LAST)
    for fed in refs[3:-1]:
        total = total + fed[...].astype(jnp.float32)
    out_ref[...] = total.astype(out_ref.dtype)


def call(kernel, args, outs, fast_out=True, raw=False, sems=0):
    ints = [x.dtype == jnp.int32 for x in args]
    space = pltpu.HBM if raw else pltpu.VMEM
    args = [
        x if flag else pltpu.with_memory_space_constraint(x, space) for x, flag in zip(args, ints)
    ]
    there = pl.BlockSpec(memory_space=space)
    return pl.pallas_call(
        kernel,
        in_specs=[SMEM if flag else there for flag in ints],
        out_specs=[VMEM] * len(outs),
        out_shape=[
            pltpu.VMEM(shape, kind) if fast_out else jax.ShapeDtypeStruct(shape, kind)
            for shape, kind in outs
        ],
        scratch_shapes=[pltpu.SemaphoreType.DMA((sems,))] if sems else [],
        compiler_params=pltpu.CompilerParams(vmem_limit_bytes=16 << 20),
    )(*args)


def few_slabs(
    slabs,
    grad_out,
    w_out,
    query_proj,
    key_proj,
    value_proj,
    w_query,
    w_key,
    w_value,
    tile_keys,
):
    rows, cols = grad_out.shape
    size = query_proj.shape[1]
    half, full = jnp.bfloat16, jnp.float32
    cut, feature_cut = rows // 2, 448

    def to_chip(x, step):
        return lax.ppermute(x, "tp", [(t, t ^ (2 * step)) for t in range(8)])

    def to_mate(x):
        return lax.ppermute(x, "tp", [(t, t ^ 1) for t in range(8)])

    def to_slab(x, turn):
        return lax.ppermute(x, "ctx", [(c, c ^ turn) for c in range(slabs)])

    def to_beside(x):
        pairs = [(c * 8 + t, (c ^ (1 + t % 2)) * 8 + t) for c in range(slabs) for t in range(8)]
        return lax.ppermute(x, ("ctx", "tp"), pairs)

    top, low = call(
        split_kernel, [grad_out], [((cut, cols), half), ((rows - cut, cols), half)],
        raw=True, sems=2,
    )
    top2 = to_chip(top, 2)
    near = to_chip(grad_out, 1)
    low2 = to_chip(low, 2)
    low3 = to_chip(low, 3)
    top3 = to_chip(top2, 1)
    pack, near_out = call(
        pack_kernel, [query_proj, key_proj, value_proj, w_out],
        [((rows, 3 * size), half), ((size, 4 * cols), half)], raw=True, sems=7,
    )
    packs = [pack] + [to_slab(pack, turn) for turn in range(1, slabs)]
    mate_out = to_mate(w_out)
    own_w = [w_query, w_key, w_value]
    mate_w = [to_mate(w) for w in own_w]
    prob_row, prob_col, attn_out = call(
        functools.partial(softmax_kernel, slabs, tile_keys.shape[1]),
        [tile_keys, *packs],
        [((rows, slabs * rows), full), ((slabs * rows, rows), full), ((slabs * rows, size), full)],
    )
    (early,) = call(
        functools.partial(attn_grad_kernel, cols, EARLY),
        [top, low, near] + ([top2, low2] if 2 in EARLY else []) + [near_out, mate_out],
        [((rows, 2 * size), full)],
    )
    late = tuple(step for step in range(4) if step not in EARLY)
    (part,) = call(
        functools.partial(attn_grad_kernel, cols, late),
        ([] if 2 in EARLY else [top2, low2]) + [top3, low3, near_out, mate_out, early],
        [((rows, 2 * size), full)],
    )
    both, grad = call(
        merge_kernel, [part, to_mate(part)],
        [((rows, 2 * size), half), ((rows, size), half)],
    )
    beside = to_beside(both)
    across = to_slab(grad, 3)
    swapped = to_mate(beside)
    (d_query,) = call(
        functools.partial(query_grad_kernel, slabs),
        [grad, *packs, prob_row, attn_out],
        [((rows, size), half)],
    )
    (own_grads,) = call(
        functools.partial(key_grad_kernel, slabs),
        [grad, beside, swapped, across, *packs, d_query, prob_col, attn_out],
        [((rows, 3 * size), half)],
    )
    mate_grads = to_mate(own_grads)
    (own_sums,) = call(
        functools.partial(project_own_kernel, cols), [own_grads, *own_w], [((4 * cols, rows), full)]
    )


    def project(step, first, count, kind, *fed):
        (part,) = call(
            functools.partial(project_kernel, cols, step, first),
            [own_sums, mate_grads, *mate_w, *fed],
            [((count, rows), kind)],
        )
        return part

    rest = cols - feature_cut
    fed = to_chip(project(3, 0, feature_cut, half), 1)
    low3 = to_chip(project(3, feature_cut, rest, half), 3)
    low2 = to_chip(project(2, feature_cut, rest, half), 2)
    near = to_chip(project(1, 0, cols, half), 1)
    top2 = to_chip(project(2, 0, feature_cut, half, fed), 2)
    own = project(0, 0, cols, full)
    through = jnp.concatenate([top2, low2], axis=0).astype(full)
    low3 = jnp.pad(low3, ((feature_cut, 0), (0, 0))).astype(full)
    out = own + near.astype(full) + through + low3
    return out


def solution(mesh):
    slabs, shards = mesh.shape["ctx"], mesh.shape["tp"]
    few = slabs == 4 and shards == 8
    return jax.shard_map(
        functools.partial(few_slabs, slabs) if few else many_slabs,
        mesh=mesh,
        in_specs=(
            P("ctx", "tp"),
            P("tp", None),
            P("ctx", "tp"),
            P("ctx", "tp"),
            P("ctx", "tp"),
            P(None, "tp"),
            P(None, "tp"),
            P(None, "tp"),
            P(),
        ),
        out_specs=P("tp", "ctx"),
        check_vma=False,
    )
```
